512 devices in a mesh: rep: 64 (over z, y), tp: 8 (over x, core).
Axes of the slice: x: 4, y: 8, z: 8, core: 2. Of those that a mesh axis runs over, the one named last changes fastest.
Arguments:
- kv_pool: bfloat16 [1024, 128, 1024], P('rep', None, 'tp'), may hold values from -6 to 6
- page_table: int32 [256, 4], P('rep'), may hold values from 0 to 15, as said below
- req_lengths: int32 [256], P('rep'), may hold values from 1 to 511, as said below
- leave_slot: int32 [64], P('rep'), may hold values from 0 to 3
- target_rep: int32 [64], P('rep'), may hold values from 0 to 63, as said below
- qkv_new: bfloat16 [256, 2560], P('rep', 'tp'), may hold values from -8.2 to 8.2
- residual_in: bfloat16 [256, 1536], P('rep'), may hold values from -6 to 6
- expert_ids: int32 [256, 4], P('rep'), may hold values from 0 to 7, all different within a row
- gate_weights: bfloat16 [256, 4], P('rep'), may hold values from 0.099609375 to 0.69921875
- norm_gain: float32 [1536], replicated, may hold values from 0.1 to 1.9
- out_proj: bfloat16 [1536, 1536], P('tp'), may hold values from -0.15625 to 0.15625
- expert_in: bfloat16 [8, 1536, 512], P('tp'), may hold values from -0.15625 to 0.15625
- expert_down: bfloat16 [8, 256, 1536], P('tp'), may hold values from -0.375 to 0.375
Outputs:
- hidden_out: bfloat16 [256, 1536], P('rep', 'tp')
- new_pages: bfloat16 [256, 128, 1024], P('rep', None, 'tp')
- arrived: bfloat16 [256, 128, 1024], P('rep', None, 'tp')
The draws below stay inside these ranges and needn't reach their ends.
Inputs may be any that keep to these rules, and one draw needn't show every extreme that they name: `req_lengths`: in every draw the request that leaves some replica has length 511. `page_table`: the 4 rows of one replica hold each of its 16 pool pages once. `target_rep`: the targets form one cycle through all replicas: every replica receives exactly one request and none keeps its own; in every draw some replica sends to the replica half the axis of replicas away.
All inputs are finite; a program needn't handle non-finite values.
Results may differ from the reference program's by a relative error of at most 0.005.
Values may be sent and summed in bfloat16 or wider, within the bound.
A program may use at most 64 MiB of HBM per device.

```python
import math
import jax
import jax.numpy as jnp
from jax import lax

D = 1536
QH = 24
KVH = 8
HD = 64
FF = 256
PAGE = 128
MAXP = 4
REQ = 4
EXPERTS = 8
TOP = 4
POOL = 16
REQS = 256
N_REP = 64


def leave_slots(key):
    return jax.random.randint(jax.random.fold_in(key, 11), (N_REP,), 0, REQ, dtype=jnp.int32)


def draw_leave_slot(key, part):
    return leave_slots(key)


def draw_target_rep(key, part):
    scores = jax.random.permutation(jax.random.fold_in(key, 13), N_REP).astype(jnp.int32)
    first = jax.random.randint(jax.random.fold_in(key, 14), (), 0, N_REP, dtype=jnp.int32)
    second = (first + N_REP // 2) % N_REP
    scores = scores.at[first].set(-2).at[second].set(-1)
    order = jnp.argsort(scores, stable=True).astype(jnp.int32)
    return jnp.zeros((N_REP,), jnp.int32).at[order].set(jnp.roll(order, -1))


def draw_req_lengths(key, part):
    limit = MAXP * PAGE
    first = jax.random.randint(jax.random.fold_in(key, 21), (REQS,), 0, limit, dtype=jnp.int32)
    second = jax.random.randint(jax.random.fold_in(key, 22), (REQS,), 0, limit, dtype=jnp.int32)
    drawn = 1 + first * second // limit
    chosen_rep = jax.random.randint(jax.random.fold_in(key, 23), (), 0, N_REP, dtype=jnp.int32)
    longest = chosen_rep * REQ + leave_slots(key)[chosen_rep]
    return drawn.at[longest].set(limit - 1)


def draw_page_table(key, part):
    table_key = jax.random.fold_in(key, 31)

    def one_replica(index):
        return jax.random.permutation(jax.random.fold_in(table_key, index), POOL)
    tables = jax.vmap(one_replica)(jnp.arange(N_REP, dtype=jnp.int32))
    return tables.reshape(REQS, MAXP).astype(jnp.int32)


def draw_kv_pool(key, part):
    full_shape = (N_REP * POOL, PAGE, KVH, 2, HD)
    drawn = jnp.clip(jax.random.normal(jax.random.fold_in(key, 42), full_shape, jnp.float32), -6.0, 6.0)
    return drawn.reshape(N_REP * POOL, PAGE, KVH * 2 * HD).astype(jnp.bfloat16)


def draw_qkv_new(key, part):
    group = QH // KVH
    full_shape = (REQS, KVH, group + 2, HD)
    drawn = jnp.clip(jax.random.normal(jax.random.fold_in(key, 51), full_shape, jnp.float32), -6.0, 6.0)
    return drawn.reshape(REQS, KVH * (group + 2) * HD).astype(jnp.bfloat16)


def level_of(key, extent, pieces, low, high):
    factor_of = 1.0
    for dim, shards_of in pieces:
        steps = jax.random.uniform(jax.random.fold_in(jax.random.fold_in(key, 6), dim), (shards_of,), jnp.float32, low / len(pieces), high / len(pieces))
        factor_of = factor_of * jnp.repeat(jnp.exp(steps), extent[dim] // shards_of).reshape((-1,) + (1,) * (len(extent) - 1 - dim))
    return factor_of


def choose_distinct(key, rows, count, top, lift):
    ranking = jax.random.permutation(jax.random.fold_in(key, 1), count)
    pull = ranking
    for power in range(3):
        pull = pull * pull // count
    pull = pull * lift // count
    tickets = jax.random.randint(jax.random.fold_in(key, 2), (rows, count), 0, 4096) + pull
    sure = jax.random.permutation(jax.random.fold_in(key, 3), rows)[jnp.arange(count) % rows]
    tickets = jnp.where(jnp.arange(rows)[:, None] == sure[None, :], 1 << 14, tickets)
    priority = tickets * count + jnp.arange(count)
    return lax.top_k(priority.astype(jnp.int32), top)[1].astype(jnp.int32)


def normal_values(rng, shape, spread, most, split=(), held_as=jnp.bfloat16):
    entries = spread * jax.random.normal(rng, shape, jnp.float32)
    if split:
        entries = entries * level_of(rng, shape, split, -0.22, 0.18)
    return jnp.clip(entries, -most, most).astype(held_as)


def setup_inputs(seed: int = 0) -> dict:
    key_of = jax.random.split(jax.random.key(seed), 14)
    kv_pool = draw_kv_pool(jax.random.fold_in(key_of[13], 71), 0)
    page_table = draw_page_table(jax.random.fold_in(key_of[13], 71), 0)
    req_lengths = draw_req_lengths(jax.random.fold_in(key_of[13], 71), 0)
    leave_slot = draw_leave_slot(jax.random.fold_in(key_of[13], 71), 0)
    target_rep = draw_target_rep(jax.random.fold_in(key_of[13], 71), 0)
    qkv_new = draw_qkv_new(jax.random.fold_in(key_of[13], 71), 0)
    residual_in = normal_values(key_of[6], (REQS, D), 1.0, 6.0, ((0, 64),))
    expert_ids = choose_distinct(key_of[7], REQS, EXPERTS, TOP, 4096)
    gate_weights = jnp.clip(0.099609375 + 0.5996094 * jax.random.uniform(key_of[8], (REQS, TOP), jnp.float32) ** level_of(key_of[8], (REQS, TOP), ((0, 64),), -0.2, 0.2), 0.099609375, 0.69921875).astype(jnp.bfloat16)
    norm_gain = jnp.clip(1.0 + 0.18 * jax.random.normal(key_of[9], (D,), jnp.float32), 0.1, 1.9)
    out_proj = normal_values(key_of[10], (QH * HD, D), (QH * HD) ** -0.5, 0.15625, ((0, 8),))
    expert_in = normal_values(key_of[11], (EXPERTS, D, 2 * FF), D ** -0.5, 0.15625, ((0, 8),))
    expert_down = normal_values(key_of[12], (EXPERTS, FF, D), FF ** -0.5, 0.375, ((0, 8),))
    return dict(kv_pool=kv_pool, page_table=page_table, req_lengths=req_lengths, leave_slot=leave_slot, target_rep=target_rep, qkv_new=qkv_new, residual_in=residual_in, expert_ids=expert_ids, gate_weights=gate_weights, norm_gain=norm_gain, out_proj=out_proj, expert_in=expert_in, expert_down=expert_down)


def reference(kv_pool, page_table, req_lengths, leave_slot, target_rep, qkv_new, residual_in, expert_ids, gate_weights, norm_gain, out_proj, expert_in, expert_down):
    group = QH // KVH
    col_total = 2 * KVH * HD
    replicas = jnp.arange(N_REP, dtype=jnp.int32)
    source_rep = jnp.zeros((N_REP,), jnp.int32).at[target_rep].set(replicas)
    global_slot = replicas * REQ + leave_slot
    anchor = jnp.arange(REQS, dtype=jnp.int32).at[global_slot].set(source_rep * REQ + leave_slot[source_rep])
    qkv_now = qkv_new[anchor]
    resid_now = residual_in[anchor]
    len_now = req_lengths[anchor]
    ids_now = expert_ids[anchor]
    gates_now = gate_weights[anchor]
    page_rows = (anchor // REQ * POOL)[:, None] + page_table[anchor]

    def per_replica(index):
        start_row = (index * REQ).astype(jnp.int32)
        rows_here = lax.dynamic_slice_in_dim(page_rows, start_row, REQ, 0)
        cache_rows = kv_pool[rows_here].reshape(REQ, MAXP * PAGE, col_total)
        qkv_here = lax.dynamic_slice_in_dim(qkv_now, start_row, REQ, 0).reshape(REQ, KVH, group + 2, HD)
        len_here = lax.dynamic_slice_in_dim(len_now, start_row, REQ, 0)
        fresh = qkv_here[:, :, group:, :].reshape(REQ, col_total)
        positions = jnp.arange(MAXP * PAGE, dtype=jnp.int32)
        at_token = positions[None, :] == len_here[:, None]
        cache_rows = jnp.where(at_token[:, :, None], fresh[:, None, :], cache_rows)
        split_cache = cache_rows.reshape(REQ, MAXP * PAGE, KVH, 2, HD).astype(jnp.float32)
        queries = qkv_here[:, :, :group, :].astype(jnp.float32)
        scores = jnp.einsum('rhgd,rlhd->rhgl', queries, split_cache[:, :, :, 0, :]) * (1.0 / math.sqrt(HD))
        visible = positions[None, :] <= len_here[:, None]
        scores = jnp.where(visible[:, None, None, :], scores, -jnp.inf)
        top_score = lax.optimization_barrier(jnp.max(scores, axis=-1, keepdims=True))
        weights = jnp.exp(scores - top_score)
        probs = (weights / lax.optimization_barrier(jnp.sum(weights, axis=-1, keepdims=True))).astype(jnp.bfloat16)
        attn_here = jnp.einsum('rhgl,rlhd->rhgd', probs.astype(jnp.float32), split_cache[:, :, :, 1, :])
        attn_here = attn_here.astype(jnp.bfloat16).reshape(REQ, QH * HD)
        paged = cache_rows.reshape(REQ, MAXP, PAGE, col_total)
        page_pick = jnp.take_along_axis(paged, (len_here // PAGE)[:, None, None, None], axis=1)[:, 0]
        came_in = lax.dynamic_index_in_dim(paged, leave_slot[index], 0, keepdims=False)
        return (attn_here, page_pick, came_in)
    attn_all, pages_all, came_all = lax.map(per_replica, replicas)
    attn_out = attn_all.reshape(REQS, QH * HD)
    new_pages = pages_all.reshape(REQS, PAGE, col_total)
    arrived = came_all.reshape(N_REP * MAXP, PAGE, col_total)
    stream = resid_now.astype(jnp.float32) + jnp.dot(attn_out, out_proj, preferred_element_type=jnp.float32)
    mean_sq = lax.optimization_barrier(jnp.mean(stream * stream, axis=1, keepdims=True))
    normed = (stream * lax.rsqrt(mean_sq + 1e-05) * norm_gain).astype(jnp.bfloat16)
    expert_mix = jnp.zeros((REQS, D), jnp.float32)
    for expert in range(EXPERTS):
        route_share = lax.optimization_barrier(jnp.sum(jnp.where(ids_now == expert, gates_now.astype(jnp.float32), 0.0), axis=1))
        up_both = jnp.dot(normed, expert_in[expert], preferred_element_type=jnp.float32)
        acted = (jax.nn.silu(up_both[:, :FF]) * up_both[:, FF:]).astype(jnp.bfloat16)
        expert_mix = expert_mix + route_share[:, None] * jnp.dot(acted, expert_down[expert], preferred_element_type=jnp.float32)
    hidden_out = (stream + expert_mix).astype(jnp.bfloat16)
    return (hidden_out, new_pages, arrived)
```

```python
import functools
import math

import jax
import jax.numpy as jnp
from jax import lax
from jax.experimental import pallas as pl
from jax.experimental.pallas import tpu as pltpu
from jax.sharding import PartitionSpec as P

HD = 64
PAGE = 128
MAXP = 4
REQ = 4
GROUP = 3
LANES = 128
TILE = 16
PG = PAGE // TILE
F32 = jnp.float32
BF16 = jnp.bfloat16
MESH = pl.DeviceIdType.MESH


def dot(a, b):
    return jnp.dot(a, b, preferred_element_type=F32)


def kernel(
    nz,
    ny,
    ntp,
    pt_ref,
    len_ref,
    leave_ref,
    target_ref,
    qkv_ref,
    res_ref,
    ids_ref,
    gate_ref,
    gain_ref,
    pool_hbm,
    wo_hbm,
    win_hbm,
    wd_hbm,
    hid_out,
    newp_out,
    arr_out,
    pool,
    wo,
    win,
    wd,
    qs,
    cache,
    first_a,
    first_b,
    send_a,
    send_b,
    last_a,
    last_b,
    parts,
    stream8,
    share_out,
    share_in,
    row_y,
    row_send,
    row_z,
    load_sem,
    send_sem,
    recv_sem,
):
    rep = lax.axis_index("rep")
    tp = lax.axis_index("tp")
    z = lax.div(rep, ny)
    y = lax.rem(rep, ny)

    def on_y(step):
        return {"rep": z * ny + lax.rem(y + step, ny)}

    def on_z(step):
        return {"rep": lax.rem(z + step, nz) * ny + y}

    def on_tp(step):
        return {"tp": lax.rem(tp + step, ntp)}

    loads = [
        pltpu.make_async_copy(pool_hbm, pool, load_sem.at[0]),
        pltpu.make_async_copy(wo_hbm, wo, load_sem.at[1]),
        pltpu.make_async_copy(win_hbm.at[0], win, load_sem.at[2]),
        pltpu.make_async_copy(wd_hbm.at[0], wd, load_sem.at[3]),
    ]
    for copy in loads:
        copy.start()

    barrier = pltpu.get_barrier_semaphore()
    for peer, count in ((on_y, ny), (on_z, nz), (on_tp, ntp)):
        for step in range(1, count):
            pl.semaphore_signal(barrier, inc=1, device_id=peer(step), device_id_type=MESH)

    def push(kind, step, src, dst, peer):
        copy = pltpu.make_async_remote_copy(
            src_ref=src,
            dst_ref=dst,
            send_sem=send_sem.at[kind, step],
            recv_sem=recv_sem.at[kind, step],
            device_id=peer(step),
            device_id_type=MESH,
        )
        copy.start()
        return copy

    leave = leave_ref[0]
    target = target_ref[0]
    low = lax.broadcasted_iota(jnp.int32, (8, LANES), 1) < HD
    qs[...] = jnp.zeros_like(qs)
    qs[0:REQ, 0 : (GROUP + 2) * HD] = qkv_ref[...].astype(F32)
    qkv_a, qkv_b, qkv_c = qs[:, 0:128], qs[:, 128:256], qs[:, 256:384]
    zero8 = jnp.zeros((8, LANES), F32)
    queries = jnp.concatenate(
        [
            jnp.where(low, qkv_a, zero8),
            jnp.where(low, pltpu.roll(qkv_a, HD, 1), zero8),
            jnp.where(low, qkv_b, zero8),
        ],
        axis=0,
    ).astype(BF16)
    fresh = jnp.where(low, pltpu.roll(qkv_b, HD, 1), pltpu.roll(qkv_c, HD, 1))

    loads[0].wait()
    row_in_page = lax.broadcasted_iota(jnp.int32, (PAGE, LANES), 0)
    for r in range(REQ):
        new_row = fresh[r : r + 1, :]
        for p in range(MAXP):
            page = pool[pt_ref[r, p]].astype(F32)
            at_token = row_in_page == len_ref[r] - p * PAGE
            cache[r, p] = jnp.where(at_token, new_row, page).astype(BF16)

    header = jnp.full((TILE, LANES), target, jnp.int32).astype(F32).astype(BF16)
    for buf, p0 in ((first_a, 0), (first_b, 2)):
        for i in range(2):
            buf[0, i * PG : (i + 1) * PG] = cache[leave, p0 + i].reshape(PG, TILE, LANES)
        buf[0, 2 * PG] = header

    pl.semaphore_wait(barrier, ny - 1 + nz - 1 + ntp - 1)
    gather_a = [push(0, d, first_a.at[0], first_a.at[d], on_y) for d in range(1, ny)]
    gather_b = [push(1, d, first_b.at[0], first_b.at[d], on_z) for d in range(1, nz)]

    span = MAXP * PAGE
    row_req = lax.broadcasted_iota(jnp.int32, (GROUP * 8, span), 0) & 7
    position = lax.broadcasted_iota(jnp.int32, (GROUP * 8, span), 1)
    scores = jnp.zeros((GROUP * 8, span), F32)
    limit = jnp.zeros((GROUP * 8, span), jnp.int32)
    for r in range(REQ):
        rows = cache[r].reshape(span, LANES)
        one = lax.dot_general(
            queries, rows, (((1,), (1,)), ((), ())), preferred_element_type=F32
        )
        scores = jnp.where(row_req == r, one, scores)
        limit = jnp.where(row_req == r, len_ref[r], limit)
    scores = jnp.where(position <= limit, scores * (1.0 / math.sqrt(HD)), -jnp.inf)
    weights = jnp.exp(scores - jnp.max(scores, axis=1, keepdims=True))
    probs = weights / jnp.sum(weights, axis=1, keepdims=True)
    attn = jnp.zeros((GROUP * 8, LANES), F32)
    for r in range(REQ):
        rows = cache[r].reshape(span, LANES)
        attn = attn + dot(jnp.where(row_req == r, probs, 0.0).astype(BF16), rows)
    heads01 = jnp.where(low, pltpu.roll(attn[0:8], HD, 1), attn[8:16]).astype(BF16)
    head2 = pltpu.roll(attn[16:24], HD, 1)[:, 0:HD].astype(BF16)
    loads[1].wait()
    part = dot(heads01, wo[0:LANES, :]) + dot(head2, wo[LANES : LANES + HD, :])
    parts[0] = part[0:REQ]
    sum_heads = [push(2, d, parts.at[0], parts.at[d], on_tp) for d in range(1, ntp)]

    share = jnp.sum(
        jnp.where(ids_ref[...] == tp, gate_ref[...].astype(F32), 0.0), axis=1, keepdims=True
    )
    total = res_ref[...].astype(F32) + parts[0]
    for d in range(1, ntp):
        sum_heads[d - 1].wait_recv()
        total = total + parts[d]
    stream8[...] = jnp.zeros_like(stream8)
    stream8[0:REQ, :] = total
    stream = stream8[...]
    mean_sq = jnp.mean(stream * stream, axis=1, keepdims=True)
    normed = (stream * lax.rsqrt(mean_sq + 1e-05) * gain_ref[...]).astype(BF16)
    loads[2].wait()
    up = dot(normed, win[...])
    half = up.shape[1] // 2
    gate, lift = up[:, 0:half], up[:, half:]
    acted = (gate * (1.0 / (1.0 + jnp.exp(-gate))) * lift).astype(BF16)
    loads[3].wait()
    down = dot(acted, wd[...])
    stream8[0:REQ, :] = down[0:REQ] * share + jnp.where(tp == 0, 1.0, 0.0) * total
    cols = stream8.shape[1] // ntp
    for t in range(ntp):
        start = t * cols // LANES * LANES
        window = stream8[:, start : start + 2 * LANES]
        if t * cols != start:
            window = jnp.concatenate(
                [
                    jnp.where(
                        low,
                        pltpu.roll(window[:, 0:LANES], HD, 1),
                        pltpu.roll(window[:, LANES:], HD, 1),
                    ),
                    pltpu.roll(window[:, LANES:], HD, 1),
                ],
                axis=1,
            )
        share_out[t] = window
    sum_experts = [
        push(3, d, share_out.at[lax.rem(tp + d, ntp)], share_in.at[d], on_tp)
        for d in range(1, ntp)
    ]

    def forward(first, send, last, waits, kind, peer, count, number_of):
        for copy in waits:
            copy.wait_recv()
        heads = [first[d, 2 * PG].astype(F32) for d in range(len(waits) + 1)]
        sent = []
        for e in range(count):
            wanted = number_of(e).astype(F32)
            packet = jnp.zeros((2 * PG, TILE, LANES), BF16)
            for d, head in enumerate(heads):
                mine = jnp.where(head == wanted, 1.0, 0.0).astype(BF16)
                packet = packet + first[d, 0 : 2 * PG] * mine[None]
            if e == 0:
                last[0] = packet
            else:
                send[e] = packet
                sent.append(push(kind, e, send.at[e], last.at[e], peer))
        return sent

    def number_z(e):
        return lax.rem(z + e, nz) * ny + y

    def number_y(e):
        return z * ny + lax.rem(y + e, ny)

    scatter_a = forward(first_a, send_a, last_a, gather_a, 4, on_z, nz, number_z)
    scatter_b = forward(first_b, send_b, last_b, gather_b, 5, on_y, ny, number_y)

    hidden = share_out[tp]
    for d in range(1, ntp):
        sum_experts[d - 1].wait_recv()
        hidden = hidden + share_in[d]
    row8 = lax.broadcasted_iota(jnp.int32, hidden.shape, 0)
    leaving = jnp.sum(jnp.where(row8 == leave, hidden, 0.0), axis=0, keepdims=True)
    page_no = lax.shift_right_logical(len_ref[leave], 7)
    row_y[0] = jnp.where(
        row8 == 0,
        leaving,
        jnp.where(row8 == 1, target, jnp.where(row8 == 2, page_no, 0)).astype(F32),
    )
    rows_y = [push(6, d, row_y.at[0], row_y.at[d], on_y) for d in range(1, ny)]
    for copy in rows_y:
        copy.wait_recv()
    rows_z = []
    for e in range(nz):
        wanted = number_z(e).astype(F32)
        message = jnp.zeros(hidden.shape, F32)
        for d in range(ny):
            one = row_y[d]
            message = message + jnp.where(one[1:2, :] == wanted, 1.0, 0.0) * one
        if e == 0:
            row_z[0] = message
        else:
            row_send[e] = message
            rows_z.append(push(7, e, row_send.at[e], row_z.at[e], on_z))
    message = row_z[0]
    for e in range(1, nz):
        rows_z[e - 1].wait_recv()
        message = message + row_z[e]
    hidden = jnp.where(row8 == leave, message[0:1, :], hidden)
    hid_out[...] = hidden[0:REQ, 0:cols].astype(BF16)

    came_page = jnp.broadcast_to(message[2:3, 0:LANES], (TILE, LANES))
    moved = jnp.zeros((PG, TILE, LANES), BF16)
    for last, waits, p0 in ((last_a, scatter_a, 0), (last_b, scatter_b, 2)):
        came = last[0]
        for e in range(1, len(waits) + 1):
            waits[e - 1].wait_recv()
            came = came + last[e]
        for i in range(2):
            page = came[i * PG : (i + 1) * PG]
            arr_out[p0 + i] = page.reshape(PAGE, LANES)
            mine = jnp.where(came_page == float(p0 + i), 1.0, 0.0).astype(BF16)
            moved = moved + page * mine[None]
    for r in range(REQ):
        kept = jnp.full((TILE, LANES), jnp.where(leave == r, 0.0, 1.0), F32)
        stays = cache[r, lax.shift_right_logical(len_ref[r], 7)].reshape(PG, TILE, LANES)
        page = stays * kept.astype(BF16)[None] + moved * (1.0 - kept).astype(BF16)[None]
        newp_out[r] = page.reshape(PAGE, LANES)

    for copies in (
        gather_a,
        gather_b,
        sum_heads,
        sum_experts,
        scatter_a,
        scatter_b,
        rows_y,
        rows_z,
    ):
        for copy in copies:
            copy.wait_send()


def local(
    nz,
    ny,
    ntp,
    kv_pool,
    page_table,
    req_lengths,
    leave_slot,
    target_rep,
    qkv_new,
    residual_in,
    expert_ids,
    gate_weights,
    norm_gain,
    out_proj,
    expert_in,
    expert_down,
):
    width = residual_in.shape[1]
    cols = width // ntp
    most = max(nz, ny, ntp)
    smem = pl.BlockSpec(memory_space=pltpu.SMEM)
    vmem = pl.BlockSpec(memory_space=pltpu.VMEM)
    hbm = pl.BlockSpec(memory_space=pl.ANY)
    return pl.pallas_call(
        functools.partial(kernel, nz, ny, ntp),
        out_shape=(
            jax.ShapeDtypeStruct((REQ, cols), BF16),
            jax.ShapeDtypeStruct((REQ, PAGE, LANES), BF16),
            jax.ShapeDtypeStruct((MAXP, PAGE, LANES), BF16),
        ),
        in_specs=[smem] * 4 + [vmem] * 5 + [hbm] * 4,
        out_specs=(vmem, vmem, vmem),
        scratch_shapes=[
            pltpu.VMEM(kv_pool.shape, BF16),
            pltpu.VMEM(out_proj.shape, BF16),
            pltpu.VMEM(expert_in.shape[1:], BF16),
            pltpu.VMEM(expert_down.shape[1:], BF16),
            pltpu.VMEM((8, 3 * LANES), F32),
            pltpu.VMEM((REQ, MAXP, PAGE, LANES), BF16),
            pltpu.VMEM((ny, 2 * PG + 1, TILE, LANES), BF16),
            pltpu.VMEM((nz, 2 * PG + 1, TILE, LANES), BF16),
            pltpu.VMEM((nz, 2 * PG, TILE, LANES), BF16),
            pltpu.VMEM((ny, 2 * PG, TILE, LANES), BF16),
            pltpu.VMEM((nz, 2 * PG, TILE, LANES), BF16),
            pltpu.VMEM((ny, 2 * PG, TILE, LANES), BF16),
            pltpu.VMEM((ntp, REQ, width), F32),
            pltpu.VMEM((8, width), F32),
            pltpu.VMEM((ntp, 8, 2 * LANES), F32),
            pltpu.VMEM((ntp, 8, 2 * LANES), F32),
            pltpu.VMEM((ny, 8, 2 * LANES), F32),
            pltpu.VMEM((nz, 8, 2 * LANES), F32),
            pltpu.VMEM((nz, 8, 2 * LANES), F32),
            pltpu.SemaphoreType.DMA((4,)),
            pltpu.SemaphoreType.DMA((8, most)),
            pltpu.SemaphoreType.DMA((8, most)),
        ],
        compiler_params=pltpu.CompilerParams(
            collective_id=0, has_side_effects=True, vmem_limit_bytes=32 << 20
        ),
    )(
        page_table,
        req_lengths,
        leave_slot,
        target_rep,
        qkv_new,
        residual_in,
        expert_ids,
        gate_weights,
        norm_gain[None, :],
        kv_pool,
        out_proj,
        expert_in,
        expert_down,
    )


def solution(mesh):
    nrep, ntp = mesh.shape["rep"], mesh.shape["tp"]
    ny = math.isqrt(nrep)
    return jax.shard_map(
        functools.partial(local, nrep // ny, ny, ntp),
        mesh=mesh,
        in_specs=(
            P("rep", None, "tp"),
            P("rep", None),
            P("rep"),
            P("rep"),
            P("rep"),
            P("rep", "tp"),
            P("rep", None),
            P("rep", None),
            P("rep", None),
            P(),
            P("tp", None),
            P("tp", None, None),
            P("tp", None, None),
        ),
        out_specs=(P("rep", "tp"), P("rep", None, "tp"), P("rep", None, "tp")),
        check_vma=False,
    )
```

```python
import functools
import math

import jax
import jax.numpy as jnp
from jax import lax
from jax.experimental import pallas as pl
from jax.experimental.pallas import tpu as pltpu
from jax.sharding import PartitionSpec as P

HD = 64
PAGE = 128
MAXP = 4
REQ = 4
GROUP = 3
LANES = 128
TILE = 16
PG = PAGE // TILE
F32 = jnp.float32
BF16 = jnp.bfloat16
MESH = pl.DeviceIdType.MESH


def dot(a, b):
    return jnp.dot(a, b, preferred_element_type=F32)


def kernel(
    nz,
    ny,
    ntp,
    pt_hbm,
    len_hbm,
    leave_hbm,
    target_hbm,
    qkv_hbm,
    res_hbm,
    ids_hbm,
    gate_hbm,
    gain_hbm,
    pool_hbm,
    wo_hbm,
    win_hbm,
    wd_hbm,
    hid_out,
    newp_out,
    arr_out,
    pt_ref,
    len_ref,
    leave_ref,
    target_ref,
    qkv_ref,
    res_ref,
    ids_ref,
    gate_ref,
    gain_ref,
    pool,
    wo,
    win,
    wd,
    qs,
    cache,
    first_a,
    first_b,
    send_a,
    send_b,
    last_a,
    last_b,
    parts,
    stream8,
    share_out,
    share_in,
    row_y,
    row_send,
    row_z,
    load_sem,
    send_sem,
    recv_sem,
    ready_sem,
):
    rep = lax.axis_index("rep")
    tp = lax.axis_index("tp")
    z = lax.div(rep, ny)
    y = lax.rem(rep, ny)

    def on_y(step):
        return {"rep": z * ny + lax.rem(y + step, ny)}

    def on_z(step):
        return {"rep": lax.rem(z + step, nz) * ny + y}

    def on_tp(step):
        return {"tp": lax.rem(tp + step, ntp)}

    pairs = (
        (pt_hbm, pt_ref),
        (len_hbm, len_ref),
        (leave_hbm, leave_ref),
        (target_hbm, target_ref),
        (qkv_hbm, qkv_ref),
        (pool_hbm, pool),
        (wo_hbm, wo),
        (res_hbm, res_ref),
        (ids_hbm, ids_ref),
        (gate_hbm, gate_ref),
        (gain_hbm, gain_ref),
        (win_hbm.at[0], win),
        (wd_hbm.at[0], wd),
    )
    loads = [
        pltpu.make_async_copy(src, dst, load_sem.at[i]) for i, (src, dst) in enumerate(pairs)
    ]
    for copy in loads:
        copy.start()

    is_late = rep * ntp + tp == 0
    late_y = jnp.logical_and(z * ntp + tp == 0, y != 0)
    late_z = jnp.logical_and(y * ntp + tp == 0, z != 0)
    late_tp = jnp.logical_and(rep == 0, tp != 0)
    late_peer = jnp.logical_or(jnp.logical_or(late_y, late_z), late_tp)
    everyone = [
        peer(step)
        for peer, count in ((on_y, ny), (on_z, nz), (on_tp, ntp))
        for step in range(1, count)
    ]
    barrier = pltpu.get_barrier_semaphore()

    @pl.when(jnp.logical_not(is_late))
    def _():
        for device in everyone:
            pl.semaphore_signal(barrier, inc=1, device_id=device, device_id_type=MESH)

    def push(kind, step, src, dst, peer, start=None):
        copy = pltpu.make_async_remote_copy(
            src_ref=src,
            dst_ref=dst,
            send_sem=send_sem.at[kind, step],
            recv_sem=recv_sem.at[kind, step],
            device_id=peer(step),
            device_id_type=MESH,
        )
        if start is None:
            copy.start()
        else:
            pl.when(start)(copy.start)
        return copy

    for copy in loads[0:5]:
        copy.wait()
    leave = leave_ref[0]
    target = target_ref[0]
    low = lax.broadcasted_iota(jnp.int32, (8, LANES), 1) < HD
    qs[...] = jnp.zeros_like(qs)
    qs[0:REQ, 0 : (GROUP + 2) * HD] = qkv_ref[...].astype(F32)
    qkv_a, qkv_b, qkv_c = qs[:, 0:128], qs[:, 128:256], qs[:, 256:384]
    zero8 = jnp.zeros((8, LANES), F32)
    queries = jnp.concatenate(
        [
            jnp.where(low, qkv_a, zero8),
            jnp.where(low, pltpu.roll(qkv_a, HD, 1), zero8),
            jnp.where(low, qkv_b, zero8),
        ],
        axis=0,
    ).astype(BF16)
    fresh = jnp.where(low, pltpu.roll(qkv_b, HD, 1), pltpu.roll(qkv_c, HD, 1))

    loads[5].wait()
    row_in_page = lax.broadcasted_iota(jnp.int32, (PAGE, LANES), 0)
    for r in range(REQ):
        new_row = fresh[r : r + 1, :]
        for p in range(MAXP):
            page = pool[pt_ref[r, p]].astype(F32)
            at_token = row_in_page == len_ref[r] - p * PAGE
            cache[r, p] = jnp.where(at_token, new_row, page).astype(BF16)

    header = jnp.full((TILE, LANES), target, jnp.int32).astype(F32).astype(BF16)
    for buf, p0 in ((first_a, 0), (first_b, 2)):
        for i in range(2):
            buf[0, i * PG : (i + 1) * PG] = cache[leave, p0 + i].reshape(PG, TILE, LANES)
        buf[0, 2 * PG] = header

    pl.semaphore_wait(barrier, len(everyone) - late_peer.astype(jnp.int32))

    @pl.when(is_late)
    def _():
        for device in everyone:
            pl.semaphore_signal(ready_sem, inc=1, device_id=device, device_id_type=MESH)

    def not_late(flag, place, step, count):
        return jnp.logical_not(jnp.logical_and(flag, place + step == count))

    gather_a = [
        push(0, d, first_a.at[0], first_a.at[d], on_y, not_late(late_y, y, d, ny))
        for d in range(1, ny)
    ]
    gather_b = [
        push(1, d, first_b.at[0], first_b.at[d], on_z, not_late(late_z, z, d, nz))
        for d in range(1, nz)
    ]

    span = MAXP * PAGE
    row_req = lax.broadcasted_iota(jnp.int32, (GROUP * 8, span), 0) & 7
    position = lax.broadcasted_iota(jnp.int32, (GROUP * 8, span), 1)
    scores = jnp.zeros((GROUP * 8, span), F32)
    limit = jnp.zeros((GROUP * 8, span), jnp.int32)
    for r in range(REQ):
        rows = cache[r].reshape(span, LANES)
        one = lax.dot_general(
            queries, rows, (((1,), (1,)), ((), ())), preferred_element_type=F32
        )
        scores = jnp.where(row_req == r, one, scores)
        limit = jnp.where(row_req == r, len_ref[r], limit)
    scores = jnp.where(position <= limit, scores * (1.0 / math.sqrt(HD)), -jnp.inf)
    weights = jnp.exp(scores - jnp.max(scores, axis=1, keepdims=True))
    probs = weights / jnp.sum(weights, axis=1, keepdims=True)
    attn = jnp.zeros((GROUP * 8, LANES), F32)
    for r in range(REQ):
        rows = cache[r].reshape(span, LANES)
        attn = attn + dot(jnp.where(row_req == r, probs, 0.0).astype(BF16), rows)
    heads01 = jnp.where(low, pltpu.roll(attn[0:8], HD, 1), attn[8:16]).astype(BF16)
    head2 = pltpu.roll(attn[16:24], HD, 1)[:, 0:HD].astype(BF16)
    loads[6].wait()
    part = dot(heads01, wo[0:LANES, :]) + dot(head2, wo[LANES : LANES + HD, :])
    parts[0] = part[0:REQ]

    @pl.when(late_peer)
    def _():
        pl.semaphore_wait(ready_sem, 1)

    @pl.when(late_y)
    def _():
        push(0, ny - y, first_a.at[0], first_a.at[ny - y], on_y)

    @pl.when(late_z)
    def _():
        push(1, nz - z, first_b.at[0], first_b.at[nz - z], on_z)

    sum_heads = [push(2, d, parts.at[0], parts.at[d], on_tp) for d in range(1, ntp)]

    for copy in loads[7:11]:
        copy.wait()
    share = jnp.sum(
        jnp.where(ids_ref[...] == tp, gate_ref[...].astype(F32), 0.0), axis=1, keepdims=True
    )
    total = res_ref[...].astype(F32) + parts[0]
    for d in range(1, ntp):
        sum_heads[d - 1].wait_recv()
        total = total + parts[d]
    stream8[...] = jnp.zeros_like(stream8)
    stream8[0:REQ, :] = total
    stream = stream8[...]
    mean_sq = jnp.mean(stream * stream, axis=1, keepdims=True)
    normed = (stream * lax.rsqrt(mean_sq + 1e-05) * gain_ref[...][None, :]).astype(BF16)
    loads[11].wait()
    up = dot(normed, win[...])
    half = up.shape[1] // 2
    gate, lift = up[:, 0:half], up[:, half:]
    acted = (gate * (1.0 / (1.0 + jnp.exp(-gate))) * lift).astype(BF16)
    loads[12].wait()
    down = dot(acted, wd[...])
    stream8[0:REQ, :] = down[0:REQ] * share + jnp.where(tp == 0, 1.0, 0.0) * total
    cols = stream8.shape[1] // ntp
    for t in range(ntp):
        start = t * cols // LANES * LANES
        window = stream8[:, start : start + 2 * LANES]
        if t * cols != start:
            window = jnp.concatenate(
                [
                    jnp.where(
                        low,
                        pltpu.roll(window[:, 0:LANES], HD, 1),
                        pltpu.roll(window[:, LANES:], HD, 1),
                    ),
                    pltpu.roll(window[:, LANES:], HD, 1),
                ],
                axis=1,
            )
        share_out[t] = window
    sum_experts = [
        push(3, d, share_out.at[lax.rem(tp + d, ntp)], share_in.at[d], on_tp)
        for d in range(1, ntp)
    ]

    def forward(first, send, last, waits, kind, peer, count, number_of):
        for copy in waits:
            copy.wait_recv()
        heads = [first[d, 2 * PG].astype(F32) for d in range(len(waits) + 1)]
        sent = []
        for e in range(count):
            wanted = number_of(e).astype(F32)
            packet = jnp.zeros((2 * PG, TILE, LANES), BF16)
            for d, head in enumerate(heads):
                mine = jnp.where(head == wanted, 1.0, 0.0).astype(BF16)
                packet = packet + first[d, 0 : 2 * PG] * mine[None]
            if e == 0:
                last[0] = packet
            else:
                send[e] = packet
                sent.append(push(kind, e, send.at[e], last.at[e], peer))
        return sent

    def number_z(e):
        return lax.rem(z + e, nz) * ny + y

    def number_y(e):
        return z * ny + lax.rem(y + e, ny)

    scatter_a = forward(first_a, send_a, last_a, gather_a, 4, on_z, nz, number_z)

    hidden = share_out[tp]
    for d in range(1, ntp):
        sum_experts[d - 1].wait_recv()
        hidden = hidden + share_in[d]
    row8 = lax.broadcasted_iota(jnp.int32, hidden.shape, 0)
    leaving = jnp.sum(jnp.where(row8 == leave, hidden, 0.0), axis=0, keepdims=True)
    page_no = lax.shift_right_logical(len_ref[leave], 7)
    row_y[0] = jnp.where(
        row8 == 0,
        leaving,
        jnp.where(row8 == 1, target, jnp.where(row8 == 2, page_no, 0)).astype(F32),
    )
    rows_y = [push(6, d, row_y.at[0], row_y.at[d], on_y) for d in range(1, ny)]
    scatter_b = forward(first_b, send_b, last_b, gather_b, 5, on_y, ny, number_y)
    for copy in rows_y:
        copy.wait_recv()
    rows_z = []
    for e in range(nz):
        wanted = number_z(e).astype(F32)
        message = jnp.zeros(hidden.shape, F32)
        for d in range(ny):
            one = row_y[d]
            message = message + jnp.where(one[1:2, :] == wanted, 1.0, 0.0) * one
        if e == 0:
            row_z[0] = message
        else:
            row_send[e] = message
            rows_z.append(push(7, e, row_send.at[e], row_z.at[e], on_z))
    message = row_z[0]
    for e in range(1, nz):
        rows_z[e - 1].wait_recv()
        message = message + row_z[e]
    hidden = jnp.where(row8 == leave, message[0:1, :], hidden)
    hid_out[...] = hidden[0:REQ, 0:cols].astype(BF16)

    came_page = jnp.broadcast_to(message[2:3, 0:LANES], (TILE, LANES))
    moved = jnp.zeros((PG, TILE, LANES), BF16)
    for last, waits, p0 in ((last_a, scatter_a, 0), (last_b, scatter_b, 2)):
        came = last[0]
        for e in range(1, len(waits) + 1):
            waits[e - 1].wait_recv()
            came = came + last[e]
        for i in range(2):
            page = came[i * PG : (i + 1) * PG]
            arr_out[p0 + i] = page.reshape(PAGE, LANES)
            mine = jnp.where(came_page == float(p0 + i), 1.0, 0.0).astype(BF16)
            moved = moved + page * mine[None]
    for r in range(REQ):
        kept = jnp.full((TILE, LANES), jnp.where(leave == r, 0.0, 1.0), F32)
        stays = cache[r, lax.shift_right_logical(len_ref[r], 7)].reshape(PG, TILE, LANES)
        page = stays * kept.astype(BF16)[None] + moved * (1.0 - kept).astype(BF16)[None]
        newp_out[r] = page.reshape(PAGE, LANES)

    for copies in (
        gather_a,
        gather_b,
        sum_heads,
        sum_experts,
        scatter_a,
        scatter_b,
        rows_y,
        rows_z,
    ):
        for copy in copies:
            copy.wait_send()


def write_out(hid, newp, arr, hid_hbm, newp_hbm, arr_hbm, sem):
    copies = [
        pltpu.make_async_copy(src, dst, sem.at[i])
        for i, (src, dst) in enumerate(((hid, hid_hbm), (newp, newp_hbm), (arr, arr_hbm)))
    ]
    for copy in copies:
        copy.start()
    for copy in copies:
        copy.wait()


def local(
    nz,
    ny,
    ntp,
    kv_pool,
    page_table,
    req_lengths,
    leave_slot,
    target_rep,
    qkv_new,
    residual_in,
    expert_ids,
    gate_weights,
    norm_gain,
    out_proj,
    expert_in,
    expert_down,
):
    width = residual_in.shape[1]
    cols = width // ntp
    most = max(nz, ny, ntp)
    vmem = pl.BlockSpec(memory_space=pltpu.VMEM)
    hbm = pl.BlockSpec(memory_space=pltpu.HBM)
    shapes = ((REQ, cols), (REQ, PAGE, LANES), (MAXP, PAGE, LANES))
    results = pl.pallas_call(
        functools.partial(kernel, nz, ny, ntp),
        out_shape=tuple(pltpu.VMEM(s, BF16) for s in shapes),
        in_specs=[hbm] * 13,
        out_specs=(vmem, vmem, vmem),
        scratch_shapes=[
            pltpu.SMEM(page_table.shape, jnp.int32),
            pltpu.SMEM(req_lengths.shape, jnp.int32),
            pltpu.SMEM(leave_slot.shape, jnp.int32),
            pltpu.SMEM(target_rep.shape, jnp.int32),
            pltpu.VMEM(qkv_new.shape, BF16),
            pltpu.VMEM(residual_in.shape, BF16),
            pltpu.VMEM(expert_ids.shape, jnp.int32),
            pltpu.VMEM(gate_weights.shape, BF16),
            pltpu.VMEM(norm_gain.shape, F32),
            pltpu.VMEM(kv_pool.shape, BF16),
            pltpu.VMEM(out_proj.shape, BF16),
            pltpu.VMEM(expert_in.shape[1:], BF16),
            pltpu.VMEM(expert_down.shape[1:], BF16),
            pltpu.VMEM((8, 3 * LANES), F32),
            pltpu.VMEM((REQ, MAXP, PAGE, LANES), BF16),
            pltpu.VMEM((ny, 2 * PG + 1, TILE, LANES), BF16),
            pltpu.VMEM((nz, 2 * PG + 1, TILE, LANES), BF16),
            pltpu.VMEM((nz, 2 * PG, TILE, LANES), BF16),
            pltpu.VMEM((ny, 2 * PG, TILE, LANES), BF16),
            pltpu.VMEM((nz, 2 * PG, TILE, LANES), BF16),
            pltpu.VMEM((ny, 2 * PG, TILE, LANES), BF16),
            pltpu.VMEM((ntp, REQ, width), F32),
            pltpu.VMEM((8, width), F32),
            pltpu.VMEM((ntp, 8, 2 * LANES), F32),
            pltpu.VMEM((ntp, 8, 2 * LANES), F32),
            pltpu.VMEM((ny, 8, 2 * LANES), F32),
            pltpu.VMEM((nz, 8, 2 * LANES), F32),
            pltpu.VMEM((nz, 8, 2 * LANES), F32),
            pltpu.SemaphoreType.DMA((13,)),
            pltpu.SemaphoreType.DMA((8, most)),
            pltpu.SemaphoreType.DMA((8, most)),
            pltpu.SemaphoreType.REGULAR,
        ],
        compiler_params=pltpu.CompilerParams(
            collective_id=0, has_side_effects=True, vmem_limit_bytes=60 << 20
        ),
    )(
        page_table,
        req_lengths,
        leave_slot,
        target_rep,
        qkv_new,
        residual_in,
        expert_ids,
        gate_weights,
        norm_gain,
        kv_pool,
        out_proj,
        expert_in,
        expert_down,
    )
    return pl.pallas_call(
        write_out,
        out_shape=tuple(jax.ShapeDtypeStruct(s, BF16) for s in shapes),
        in_specs=[vmem] * 3,
        out_specs=[hbm] * 3,
        scratch_shapes=[pltpu.SemaphoreType.DMA((3,))],
        compiler_params=pltpu.CompilerParams(vmem_limit_bytes=1 << 20),
    )(*results)


def solution(mesh):
    nrep, ntp = mesh.shape["rep"], mesh.shape["tp"]
    ny = math.isqrt(nrep)
    return jax.shard_map(
        functools.partial(local, nrep // ny, ny, ntp),
        mesh=mesh,
        in_specs=(
            P("rep", None, "tp"),
            P("rep", None),
            P("rep"),
            P("rep"),
            P("rep"),
            P("rep", "tp"),
            P("rep", None),
            P("rep", None),
            P("rep", None),
            P(),
            P("tp", None),
            P("tp", None, None),
            P("tp", None, None),
        ),
        out_specs=(P("rep", "tp"), P("rep", None, "tp"), P("rep", None, "tp")),
        check_vma=False,
    )
```

```python
import functools
import math

import jax
import jax.numpy as jnp
from jax import lax
from jax.experimental import pallas as pl
from jax.experimental.pallas import tpu as pltpu
from jax.sharding import PartitionSpec as P

HD = 64
PAGE = 128
MAXP = 4
REQ = 4
GROUP = 3
LANES = 128
TILE = 16
PG = PAGE // TILE
F32 = jnp.float32
BF16 = jnp.bfloat16
MESH = pl.DeviceIdType.MESH


def dot(a, b):
    return jnp.dot(a, b, preferred_element_type=F32)


def kernel(
    nz,
    ny,
    ntp,
    pt_hbm,
    len_hbm,
    leave_hbm,
    target_hbm,
    qkv_hbm,
    res_hbm,
    ids_hbm,
    gate_hbm,
    gain_hbm,
    pool_hbm,
    wo_hbm,
    win_hbm,
    wd_hbm,
    hid_out,
    newp_out,
    arr_out,
    pt_ref,
    len_ref,
    leave_ref,
    target_ref,
    qkv_ref,
    res_ref,
    ids_ref,
    gate_ref,
    gain_ref,
    pool,
    wo,
    win,
    wd,
    qs,
    cache,
    first_a,
    first_b,
    send_a,
    send_b,
    last_a,
    last_b,
    hops_a,
    hops_b,
    parts,
    stream8,
    share_out,
    share_in,
    row_y,
    row_send,
    row_z,
    load_sem,
    send_sem,
    recv_sem,
    ready_sem,
):
    rep = lax.axis_index("rep")
    tp = lax.axis_index("tp")
    z = lax.div(rep, ny)
    y = lax.rem(rep, ny)

    def on_y(step):
        return {"rep": z * ny + lax.rem(y + step, ny)}

    def on_z(step):
        return {"rep": lax.rem(z + step, nz) * ny + y}

    def on_tp(step):
        return {"tp": lax.rem(tp + step, ntp)}

    pairs = (
        (pt_hbm, pt_ref),
        (len_hbm, len_ref),
        (leave_hbm, leave_ref),
        (target_hbm, target_ref),
        (qkv_hbm, qkv_ref),
        (pool_hbm, pool),
        (wo_hbm, wo),
        (res_hbm, res_ref),
        (ids_hbm, ids_ref),
        (gate_hbm, gate_ref),
        (gain_hbm, gain_ref),
        (win_hbm.at[0], win),
        (wd_hbm.at[0], wd),
    )
    loads = [
        pltpu.make_async_copy(src, dst, load_sem.at[i]) for i, (src, dst) in enumerate(pairs)
    ]
    for copy in loads:
        copy.start()

    is_late = rep * ntp + tp == 0
    late_y = jnp.logical_and(z * ntp + tp == 0, y != 0)
    late_z = jnp.logical_and(y * ntp + tp == 0, z != 0)
    late_tp = jnp.logical_and(rep == 0, tp != 0)
    late_peer = jnp.logical_or(jnp.logical_or(late_y, late_z), late_tp)
    everyone = [
        peer(step)
        for peer, count in ((on_y, ny), (on_z, nz), (on_tp, ntp))
        for step in range(1, count)
    ]
    barrier = pltpu.get_barrier_semaphore()

    @pl.when(jnp.logical_not(is_late))
    def _():
        for device in everyone:
            pl.semaphore_signal(barrier, inc=1, device_id=device, device_id_type=MESH)

    def push(kind, sem, src, dst, device, start=None):
        copy = pltpu.make_async_remote_copy(
            src_ref=src,
            dst_ref=dst,
            send_sem=send_sem.at[kind, sem],
            recv_sem=recv_sem.at[kind, sem],
            device_id=device,
            device_id_type=MESH,
        )
        if start is None:
            copy.start()
        else:
            pl.when(start)(copy.start)
        return copy

    for copy in loads[0:5]:
        copy.wait()
    leave = leave_ref[0]
    target = target_ref[0]
    low = lax.broadcasted_iota(jnp.int32, (8, LANES), 1) < HD
    qs[...] = jnp.zeros_like(qs)
    qs[0:REQ, 0 : (GROUP + 2) * HD] = qkv_ref[...].astype(F32)
    qkv_a, qkv_b, qkv_c = qs[:, 0:128], qs[:, 128:256], qs[:, 256:384]
    zero8 = jnp.zeros((8, LANES), F32)
    queries = jnp.concatenate(
        [
            jnp.where(low, qkv_a, zero8),
            jnp.where(low, pltpu.roll(qkv_a, HD, 1), zero8),
            jnp.where(low, qkv_b, zero8),
        ],
        axis=0,
    ).astype(BF16)
    fresh = jnp.where(low, pltpu.roll(qkv_b, HD, 1), pltpu.roll(qkv_c, HD, 1))

    loads[5].wait()
    row_in_page = lax.broadcasted_iota(jnp.int32, (PAGE, LANES), 0)
    for r in range(REQ):
        new_row = fresh[r : r + 1, :]
        for p in range(MAXP):
            page = pool[pt_ref[r, p]].astype(F32)
            at_token = row_in_page == len_ref[r] - p * PAGE
            cache[r, p] = jnp.where(at_token, new_row, page).astype(BF16)

    header = jnp.full((TILE, LANES), target, jnp.int32).astype(F32).astype(BF16)
    for buf, p0 in ((first_a, 0), (first_b, 2)):
        buf[0, 0:PG] = cache[leave, p0].reshape(PG, TILE, LANES)
        buf[0, PG] = header
        buf[0, PG + 1 :] = cache[leave, p0 + 1].reshape(PG, TILE, LANES)

    pl.semaphore_wait(barrier, len(everyone) - late_peer.astype(jnp.int32))

    @pl.when(is_late)
    def _():
        for device in everyone:
            pl.semaphore_signal(ready_sem, inc=1, device_id=device, device_id_type=MESH)

    def to_late(flag, place, step, count):
        return jnp.logical_and(flag, place + step == count)

    def spread(kind, first, peer, flag, place, count):
        near = {}
        for d in (1, 2, count - 2, count - 1):
            late = to_late(flag, place, d, count)
            near[d] = push(kind, d, first.at[0], first.at[d], peer(d), jnp.logical_not(late))
        return near

    def spread_late(near, flag, place, count):
        for d, copy in near.items():
            pl.when(to_late(flag, place, d, count))(copy.start)

    def pass_on(kind, first, peer, near):
        upper, lower = pl.ds(0, PG + 1), pl.ds(PG + 1, PG)
        near[2].wait_recv()
        far = [
            push(kind, 4, first.at[2, upper], first.at[4, upper], peer(2)),
            push(kind, 3, first.at[2], first.at[3], peer(1)),
        ]
        near[6].wait_recv()
        far += [
            push(kind, 0, first.at[6, lower], first.at[4, lower], peer(6)),
            push(kind, 5, first.at[6], first.at[5], peer(7)),
        ]
        return far

    near_a = spread(0, first_a, on_y, late_y, y, ny)
    near_b = spread(1, first_b, on_z, late_z, z, nz)

    span = MAXP * PAGE
    row_req = lax.broadcasted_iota(jnp.int32, (GROUP * 8, span), 0) & 7
    position = lax.broadcasted_iota(jnp.int32, (GROUP * 8, span), 1)
    scores = jnp.zeros((GROUP * 8, span), F32)
    limit = jnp.zeros((GROUP * 8, span), jnp.int32)
    for r in range(REQ):
        rows = cache[r].reshape(span, LANES)
        one = lax.dot_general(
            queries, rows, (((1,), (1,)), ((), ())), preferred_element_type=F32
        )
        scores = jnp.where(row_req == r, one, scores)
        limit = jnp.where(row_req == r, len_ref[r], limit)
    scores = jnp.where(position <= limit, scores * (1.0 / math.sqrt(HD)), -jnp.inf)
    weights = jnp.exp(scores - jnp.max(scores, axis=1, keepdims=True))
    probs = weights / jnp.sum(weights, axis=1, keepdims=True)
    attn = jnp.zeros((GROUP * 8, LANES), F32)
    for r in range(REQ):
        rows = cache[r].reshape(span, LANES)
        attn = attn + dot(jnp.where(row_req == r, probs, 0.0).astype(BF16), rows)
    heads01 = jnp.where(low, pltpu.roll(attn[0:8], HD, 1), attn[8:16]).astype(BF16)
    head2 = pltpu.roll(attn[16:24], HD, 1)[:, 0:HD].astype(BF16)
    loads[6].wait()
    part = dot(heads01, wo[0:LANES, :]) + dot(head2, wo[LANES : LANES + HD, :])
    parts[0] = part[0:REQ]

    @pl.when(late_peer)
    def _():
        pl.semaphore_wait(ready_sem, 1)

    spread_late(near_a, late_y, y, ny)
    spread_late(near_b, late_z, z, nz)
    sum_heads = [push(2, d, parts.at[0], parts.at[d], on_tp(d)) for d in range(1, ntp)]

    far_a = pass_on(0, first_a, on_y, near_a)
    far_b = pass_on(1, first_b, on_z, near_b)

    for copy in loads[7:11]:
        copy.wait()
    share = jnp.sum(
        jnp.where(ids_ref[...] == tp, gate_ref[...].astype(F32), 0.0), axis=1, keepdims=True
    )
    total = res_ref[...].astype(F32) + parts[0]
    for d in range(1, ntp):
        sum_heads[d - 1].wait_recv()
        total = total + parts[d]
    stream8[...] = jnp.zeros_like(stream8)
    stream8[0:REQ, :] = total
    stream = stream8[...]
    mean_sq = jnp.mean(stream * stream, axis=1, keepdims=True)
    normed = (stream * lax.rsqrt(mean_sq + 1e-05) * gain_ref[...][None, :]).astype(BF16)
    loads[11].wait()
    up = dot(normed, win[...])
    half = up.shape[1] // 2
    gate, lift = up[:, 0:half], up[:, half:]
    acted = (gate * (1.0 / (1.0 + jnp.exp(-gate))) * lift).astype(BF16)
    loads[12].wait()
    down = dot(acted, wd[...])
    stream8[0:REQ, :] = down[0:REQ] * share + jnp.where(tp == 0, 1.0, 0.0) * total
    cols = stream8.shape[1] // ntp
    for t in range(ntp):
        start = t * cols // LANES * LANES
        window = stream8[:, start : start + 2 * LANES]
        if t * cols != start:
            window = jnp.concatenate(
                [
                    jnp.where(
                        low,
                        pltpu.roll(window[:, 0:LANES], HD, 1),
                        pltpu.roll(window[:, LANES:], HD, 1),
                    ),
                    pltpu.roll(window[:, LANES:], HD, 1),
                ],
                axis=1,
            )
        share_out[t] = window
    sum_experts = [
        push(3, d, share_out.at[lax.rem(tp + d, ntp)], share_in.at[d], on_tp(d))
        for d in range(1, ntp)
    ]

    def scatter(first, near, far, send, last, hops, kind, peer, number_of):
        near[1].wait_recv()
        near[7].wait_recv()
        for copy in far:
            copy.wait_recv()
        heads = [first[d, PG].astype(F32) for d in range(8)]

        def packet(e, out):
            wanted = number_of(e).astype(F32)
            upper = jnp.zeros((PG, TILE, LANES), BF16)
            lower = upper
            for d, head in enumerate(heads):
                mine = jnp.where(head == wanted, 1.0, 0.0).astype(BF16)[None]
                upper = upper + first[d, 0:PG] * mine
                lower = lower + first[d, PG + 1 :] * mine
            out[0:PG] = upper
            out[PG:] = lower

        def send_to(e, sem, src, dst):
            return push(kind, sem, src, dst, peer(e))

        packet(4, send.at[4])
        sent = {
            4: send_to(2, 4, send.at[4, pl.ds(0, PG)], hops.at[2, pl.ds(0, PG)]),
            0: send_to(6, 0, send.at[4, pl.ds(PG, PG)], hops.at[2, pl.ds(PG, PG)]),
        }
        packet(3, send.at[3])
        sent[3] = send_to(1, 3, send.at[3], hops.at[0])
        packet(5, send.at[5])
        sent[5] = send_to(7, 5, send.at[5], hops.at[1])
        for e in (1, 7):
            packet(e, send.at[e])
            sent[e] = send_to(e, e, send.at[e], last.at[e])
        for e in (2, 6):
            packet(e, send.at[e])
        packet(0, last.at[0])
        return sent

    def scatter_on(sent, send, last, hops, kind, peer):
        sent[3].wait_recv()
        sent[4].wait_recv()
        send[2] = send[2] + hops[0]
        send[2, 0:PG] = send[2, 0:PG] + hops[2, 0:PG]
        sent[2] = push(kind, 2, send.at[2], last.at[2], peer(2))
        sent[5].wait_recv()
        sent[0].wait_recv()
        send[6] = send[6] + hops[1]
        send[6, PG:] = send[6, PG:] + hops[2, PG:]
        sent[6] = push(kind, 6, send.at[6], last.at[6], peer(6))

    def number_z(e):
        return lax.rem(z + e, nz) * ny + y

    def number_y(e):
        return z * ny + lax.rem(y + e, ny)

    sent_a = scatter(first_a, near_a, far_a, send_a, last_a, hops_a, 4, on_z, number_z)

    hidden = share_out[tp]
    for d in range(1, ntp):
        sum_experts[d - 1].wait_recv()
        hidden = hidden + share_in[d]
    row8 = lax.broadcasted_iota(jnp.int32, hidden.shape, 0)
    leaving = jnp.sum(jnp.where(row8 == leave, hidden, 0.0), axis=0, keepdims=True)
    page_no = lax.shift_right_logical(len_ref[leave], 7)
    row_y[0] = jnp.where(
        row8 == 0,
        leaving,
        jnp.where(row8 == 1, target, jnp.where(row8 == 2, page_no, 0)).astype(F32),
    )
    rows_y = [push(6, d, row_y.at[0], row_y.at[d], on_y(d)) for d in range(1, ny)]
    sent_b = scatter(first_b, near_b, far_b, send_b, last_b, hops_b, 5, on_y, number_y)
    scatter_on(sent_a, send_a, last_a, hops_a, 4, on_z)
    scatter_on(sent_b, send_b, last_b, hops_b, 5, on_y)
    for copy in rows_y:
        copy.wait_recv()
    rows_z = []
    for e in range(nz):
        wanted = number_z(e).astype(F32)
        message = jnp.zeros(hidden.shape, F32)
        for d in range(ny):
            one = row_y[d]
            message = message + jnp.where(one[1:2, :] == wanted, 1.0, 0.0) * one
        if e == 0:
            row_z[0] = message
        else:
            row_send[e] = message
            rows_z.append(push(7, e, row_send.at[e], row_z.at[e], on_z(e)))
    message = row_z[0]
    for e in range(1, nz):
        rows_z[e - 1].wait_recv()
        message = message + row_z[e]
    hidden = jnp.where(row8 == leave, message[0:1, :], hidden)
    hid_out[...] = hidden[0:REQ, 0:cols].astype(BF16)

    came_page = jnp.broadcast_to(message[2:3, 0:LANES], (TILE, LANES))
    moved = jnp.zeros((PG, TILE, LANES), BF16)
    for last, sent, p0 in ((last_a, sent_a, 0), (last_b, sent_b, 2)):
        came = last[0]
        for e in (1, 7, 2, 6):
            sent[e].wait_recv()
            came = came + last[e]
        for i in range(2):
            page = came[i * PG : (i + 1) * PG]
            arr_out[p0 + i] = page.reshape(PAGE, LANES)
            mine = jnp.where(came_page == float(p0 + i), 1.0, 0.0).astype(BF16)
            moved = moved + page * mine[None]
    for r in range(REQ):
        kept = jnp.full((TILE, LANES), jnp.where(leave == r, 0.0, 1.0), F32)
        stays = cache[r, lax.shift_right_logical(len_ref[r], 7)].reshape(PG, TILE, LANES)
        page = stays * kept.astype(BF16)[None] + moved * (1.0 - kept).astype(BF16)[None]
        newp_out[r] = page.reshape(PAGE, LANES)

    for copies in (
        near_a.values(),
        near_b.values(),
        far_a,
        far_b,
        sum_heads,
        sum_experts,
        sent_a.values(),
        sent_b.values(),
        rows_y,
        rows_z,
    ):
        for copy in copies:
            copy.wait_send()


def write_out(hid, newp, arr, hid_hbm, newp_hbm, arr_hbm, sem):
    copies = [
        pltpu.make_async_copy(src, dst, sem.at[i])
        for i, (src, dst) in enumerate(((hid, hid_hbm), (newp, newp_hbm), (arr, arr_hbm)))
    ]
    for copy in copies:
        copy.start()
    for copy in copies:
        copy.wait()


def local(
    nz,
    ny,
    ntp,
    kv_pool,
    page_table,
    req_lengths,
    leave_slot,
    target_rep,
    qkv_new,
    residual_in,
    expert_ids,
    gate_weights,
    norm_gain,
    out_proj,
    expert_in,
    expert_down,
):
    width = residual_in.shape[1]
    cols = width // ntp
    most = max(nz, ny, ntp)
    vmem = pl.BlockSpec(memory_space=pltpu.VMEM)
    hbm = pl.BlockSpec(memory_space=pltpu.HBM)
    shapes = ((REQ, cols), (REQ, PAGE, LANES), (MAXP, PAGE, LANES))
    results = pl.pallas_call(
        functools.partial(kernel, nz, ny, ntp),
        out_shape=tuple(pltpu.VMEM(s, BF16) for s in shapes),
        in_specs=[hbm] * 13,
        out_specs=(vmem, vmem, vmem),
        scratch_shapes=[
            pltpu.SMEM(page_table.shape, jnp.int32),
            pltpu.SMEM(req_lengths.shape, jnp.int32),
            pltpu.SMEM(leave_slot.shape, jnp.int32),
            pltpu.SMEM(target_rep.shape, jnp.int32),
            pltpu.VMEM(qkv_new.shape, BF16),
            pltpu.VMEM(residual_in.shape, BF16),
            pltpu.VMEM(expert_ids.shape, jnp.int32),
            pltpu.VMEM(gate_weights.shape, BF16),
            pltpu.VMEM(norm_gain.shape, F32),
            pltpu.VMEM(kv_pool.shape, BF16),
            pltpu.VMEM(out_proj.shape, BF16),
            pltpu.VMEM(expert_in.shape[1:], BF16),
            pltpu.VMEM(expert_down.shape[1:], BF16),
            pltpu.VMEM((8, 3 * LANES), F32),
            pltpu.VMEM((REQ, MAXP, PAGE, LANES), BF16),
            pltpu.VMEM((ny, 2 * PG + 1, TILE, LANES), BF16),
            pltpu.VMEM((nz, 2 * PG + 1, TILE, LANES), BF16),
            pltpu.VMEM((nz, 2 * PG, TILE, LANES), BF16),
            pltpu.VMEM((ny, 2 * PG, TILE, LANES), BF16),
            pltpu.VMEM((nz, 2 * PG, TILE, LANES), BF16),
            pltpu.VMEM((ny, 2 * PG, TILE, LANES), BF16),
            pltpu.VMEM((3, 2 * PG, TILE, LANES), BF16),
            pltpu.VMEM((3, 2 * PG, TILE, LANES), BF16),
            pltpu.VMEM((ntp, REQ, width), F32),
            pltpu.VMEM((8, width), F32),
            pltpu.VMEM((ntp, 8, 2 * LANES), F32),
            pltpu.VMEM((ntp, 8, 2 * LANES), F32),
            pltpu.VMEM((ny, 8, 2 * LANES), F32),
            pltpu.VMEM((nz, 8, 2 * LANES), F32),
            pltpu.VMEM((nz, 8, 2 * LANES), F32),
            pltpu.SemaphoreType.DMA((13,)),
            pltpu.SemaphoreType.DMA((8, most)),
            pltpu.SemaphoreType.DMA((8, most)),
            pltpu.SemaphoreType.REGULAR,
        ],
        compiler_params=pltpu.CompilerParams(
            collective_id=0, has_side_effects=True, vmem_limit_bytes=60 << 20
        ),
    )(
        page_table,
        req_lengths,
        leave_slot,
        target_rep,
        qkv_new,
        residual_in,
        expert_ids,
        gate_weights,
        norm_gain,
        kv_pool,
        out_proj,
        expert_in,
        expert_down,
    )
    return pl.pallas_call(
        write_out,
        out_shape=tuple(jax.ShapeDtypeStruct(s, BF16) for s in shapes),
        in_specs=[vmem] * 3,
        out_specs=[hbm] * 3,
        scratch_shapes=[pltpu.SemaphoreType.DMA((3,))],
        compiler_params=pltpu.CompilerParams(vmem_limit_bytes=1 << 20),
    )(*results)


def solution(mesh):
    nrep, ntp = mesh.shape["rep"], mesh.shape["tp"]
    ny = math.isqrt(nrep)
    return jax.shard_map(
        functools.partial(local, nrep // ny, ny, ntp),
        mesh=mesh,
        in_specs=(
            P("rep", None, "tp"),
            P("rep", None),
            P("rep"),
            P("rep"),
            P("rep"),
            P("rep", "tp"),
            P("rep", None),
            P("rep", None),
            P("rep", None),
            P(),
            P("tp", None),
            P("tp", None, None),
            P("tp", None, None),
        ),
        out_specs=(P("rep", "tp"), P("rep", None, "tp"), P("rep", None, "tp")),
        check_vma=False,
    )
```

```python
import functools
import math

import jax
import jax.numpy as jnp
from jax import lax
from jax.experimental import pallas as pl
from jax.experimental.pallas import tpu as pltpu
from jax.sharding import PartitionSpec as P

HD = 64
PAGE = 128
MAXP = 4
REQ = 4
GROUP = 3
LANES = 128
TILE = 16
PG = PAGE // TILE
F32 = jnp.float32
BF16 = jnp.bfloat16
MESH = pl.DeviceIdType.MESH


def dot(a, b):
    return jnp.dot(a, b, preferred_element_type=F32)


def kernel(
    nz,
    ny,
    ntp,
    pt_hbm,
    len_hbm,
    leave_hbm,
    target_hbm,
    qkv_hbm,
    res_hbm,
    ids_hbm,
    gate_hbm,
    gain_hbm,
    pool_hbm,
    wo_hbm,
    win_hbm,
    wd_hbm,
    hid_out,
    newp_out,
    arr_out,
    pt_ref,
    len_ref,
    leave_ref,
    target_ref,
    qkv_ref,
    res_ref,
    ids_ref,
    gate_ref,
    gain_ref,
    pool,
    wo,
    win,
    wd,
    qs,
    new_kv,
    cache,
    first_a,
    first_b,
    send_a,
    send_b,
    last_a,
    last_b,
    hops_a,
    hops_b,
    parts,
    stream8,
    share_out,
    share_in,
    row_y,
    row_send,
    row_z,
    load_sem,
    send_sem,
    recv_sem,
    ready_sem,
):
    rep = lax.axis_index("rep")
    tp = lax.axis_index("tp")
    z = lax.div(rep, ny)
    y = lax.rem(rep, ny)

    def on_y(step):
        return {"rep": z * ny + lax.rem(y + step, ny)}

    def on_z(step):
        return {"rep": lax.rem(z + step, nz) * ny + y}

    def on_tp(step):
        return {"tp": lax.rem(tp + step, ntp)}

    pairs = (
        (pt_hbm, pt_ref),
        (len_hbm, len_ref),
        (leave_hbm, leave_ref),
        (target_hbm, target_ref),
        (qkv_hbm, qkv_ref),
        (pool_hbm, pool),
        (wo_hbm, wo),
        (res_hbm, res_ref),
        (ids_hbm, ids_ref),
        (gate_hbm, gate_ref),
        (gain_hbm, gain_ref),
        (win_hbm.at[0], win),
        (wd_hbm.at[0], wd),
    )
    loads = [
        pltpu.make_async_copy(src, dst, load_sem.at[i]) for i, (src, dst) in enumerate(pairs)
    ]
    for copy in loads[0:6]:
        copy.start()

    is_late = rep * ntp + tp == 0
    near_y = (1, 2, ny - 2, ny - 1)
    near_z = (1, 2, nz - 2, nz - 1)

    def beside(place, steps):
        hits = [place == step for step in steps]
        return functools.reduce(jnp.logical_or, hits)

    late_y = jnp.logical_and(z * ntp + tp == 0, beside(y, near_y))
    late_z = jnp.logical_and(y * ntp + tp == 0, beside(z, near_z))
    late_tp = jnp.logical_and(rep == 0, tp != 0)
    late_peer = jnp.logical_or(jnp.logical_or(late_y, late_z), late_tp)
    everyone = [
        peer(step)
        for peer, steps in ((on_y, near_y), (on_z, near_z), (on_tp, range(1, ntp)))
        for step in steps
    ]
    barrier = pltpu.get_barrier_semaphore()

    @pl.when(jnp.logical_not(is_late))
    def _():
        for device in everyone:
            pl.semaphore_signal(barrier, inc=1, device_id=device, device_id_type=MESH)

    @pl.when(is_late)
    def _():
        pl.semaphore_wait(barrier, len(everyone))
        for device in everyone:
            pl.semaphore_signal(ready_sem, inc=1, device_id=device, device_id_type=MESH)

    def push(kind, sem, src, dst, device, start=None):
        copy = pltpu.make_async_remote_copy(
            src_ref=src,
            dst_ref=dst,
            send_sem=send_sem.at[kind, sem],
            recv_sem=recv_sem.at[kind, sem],
            device_id=device,
            device_id_type=MESH,
        )
        if start is None:
            copy.start()
        else:
            pl.when(start)(copy.start)
        return copy

    for copy in loads[0:5]:
        copy.wait()
    leave = leave_ref[0]
    target = target_ref[0]
    low = lax.broadcasted_iota(jnp.int32, (8, LANES), 1) < HD
    qs[...] = jnp.zeros_like(qs)
    qs[0:REQ, 0 : (GROUP + 2) * HD] = qkv_ref[...].astype(F32)
    qkv_a, qkv_b, qkv_c = qs[:, 0:128], qs[:, 128:256], qs[:, 256:384]
    zero8 = jnp.zeros((8, LANES), F32)
    queries = jnp.concatenate(
        [
            jnp.where(low, qkv_a, zero8),
            jnp.where(low, pltpu.roll(qkv_a, HD, 1), zero8),
            jnp.where(low, qkv_b, zero8),
        ],
        axis=0,
    ).astype(BF16)
    fresh = jnp.where(low, pltpu.roll(qkv_b, HD, 1), pltpu.roll(qkv_c, HD, 1))

    loads[5].wait()
    for copy in loads[6:]:
        copy.start()
    new_kv[...] = fresh
    row_in_page = lax.broadcasted_iota(jnp.int32, (PAGE, LANES), 0)

    def with_token(r, p):
        at_token = row_in_page == len_ref[r] - p * PAGE
        page = pool[pt_ref[r, p]].astype(F32)
        return jnp.where(at_token, new_kv[pl.ds(r, 1), :], page).astype(BF16)

    header = jnp.full((TILE, LANES), target, jnp.int32).astype(F32).astype(BF16)
    for buf, p0 in ((first_a, 0), (first_b, 2)):
        buf[0, 0:PG] = with_token(leave, p0).reshape(PG, TILE, LANES)
        buf[0, PG] = header
        buf[0, PG + 1 :] = with_token(leave, p0 + 1).reshape(PG, TILE, LANES)

    @pl.when(jnp.logical_not(is_late))
    def _():
        pl.semaphore_wait(barrier, len(everyone) - late_peer.astype(jnp.int32))

    def to_late(flag, place, step, count):
        return jnp.logical_and(flag, place + step == count)

    def spread(kind, first, peer, flag, place, count):
        near = {}
        for d in (2, count - 2, 1, count - 1):
            late = to_late(flag, place, d, count)
            near[d] = push(kind, d, first.at[0], first.at[d], peer(d), jnp.logical_not(late))
        return near

    def spread_late(near, flag, place, count):
        for d, copy in near.items():
            pl.when(to_late(flag, place, d, count))(copy.start)

    def pass_on(kind, first, peer, near):
        upper, lower = pl.ds(0, PG + 1), pl.ds(PG + 1, PG)
        near[2].wait_recv()
        far = [
            push(kind, 4, first.at[2, upper], first.at[4, upper], peer(2)),
            push(kind, 3, first.at[2], first.at[3], peer(1)),
        ]
        near[6].wait_recv()
        far += [
            push(kind, 0, first.at[6, lower], first.at[4, lower], peer(6)),
            push(kind, 5, first.at[6], first.at[5], peer(7)),
        ]
        return far

    near_a = spread(0, first_a, on_y, late_y, y, ny)
    near_b = spread(1, first_b, on_z, late_z, z, nz)

    for r in range(REQ):
        for p in range(MAXP):
            cache[r, p] = with_token(r, p)

    span = MAXP * PAGE
    row_req = lax.broadcasted_iota(jnp.int32, (GROUP * 8, span), 0) & 7
    position = lax.broadcasted_iota(jnp.int32, (GROUP * 8, span), 1)
    scores = jnp.zeros((GROUP * 8, span), F32)
    limit = jnp.zeros((GROUP * 8, span), jnp.int32)
    for r in range(REQ):
        rows = cache[r].reshape(span, LANES)
        one = lax.dot_general(
            queries, rows, (((1,), (1,)), ((), ())), preferred_element_type=F32
        )
        scores = jnp.where(row_req == r, one, scores)
        limit = jnp.where(row_req == r, len_ref[r], limit)
    scores = jnp.where(position <= limit, scores * (1.0 / math.sqrt(HD)), -jnp.inf)
    weights = jnp.exp(scores - jnp.max(scores, axis=1, keepdims=True))
    probs = weights / jnp.sum(weights, axis=1, keepdims=True)
    attn = jnp.zeros((GROUP * 8, LANES), F32)
    for r in range(REQ):
        rows = cache[r].reshape(span, LANES)
        attn = attn + dot(jnp.where(row_req == r, probs, 0.0).astype(BF16), rows)
    heads01 = jnp.where(low, pltpu.roll(attn[0:8], HD, 1), attn[8:16]).astype(BF16)
    head2 = pltpu.roll(attn[16:24], HD, 1)[:, 0:HD].astype(BF16)
    loads[6].wait()
    part = dot(heads01, wo[0:LANES, :]) + dot(head2, wo[LANES : LANES + HD, :])
    parts[0] = part[0:REQ].astype(BF16)

    @pl.when(late_peer)
    def _():
        pl.semaphore_wait(ready_sem, 1)

    spread_late(near_a, late_y, y, ny)
    spread_late(near_b, late_z, z, nz)
    sum_heads = [push(2, d, parts.at[0], parts.at[d], on_tp(d)) for d in range(1, ntp)]

    far_a = pass_on(0, first_a, on_y, near_a)
    far_b = pass_on(1, first_b, on_z, near_b)

    for copy in loads[7:11]:
        copy.wait()
    share = jnp.sum(
        jnp.where(ids_ref[...] == tp, gate_ref[...].astype(F32), 0.0), axis=1, keepdims=True
    )
    total = res_ref[...].astype(F32) + part[0:REQ]
    for d in range(1, ntp):
        sum_heads[d - 1].wait_recv()
        total = total + parts[d].astype(F32)
    stream8[...] = jnp.zeros_like(stream8)
    stream8[0:REQ, :] = total
    stream = stream8[...]
    mean_sq = jnp.mean(stream * stream, axis=1, keepdims=True)
    normed = (stream * lax.rsqrt(mean_sq + 1e-05) * gain_ref[...][None, :]).astype(BF16)
    loads[11].wait()
    up = dot(normed, win[...])
    half = up.shape[1] // 2
    gate, lift = up[:, 0:half], up[:, half:]
    acted = (gate * (1.0 / (1.0 + jnp.exp(-gate))) * lift).astype(BF16)
    loads[12].wait()
    down = dot(acted, wd[...])
    stream8[0:REQ, :] = down[0:REQ] * share + jnp.where(tp == 0, 1.0, 0.0) * total
    cols = stream8.shape[1] // ntp
    for t in range(ntp):
        start = t * cols // LANES * LANES
        window = stream8[:, start : start + 2 * LANES]
        if t * cols != start:
            window = jnp.concatenate(
                [
                    jnp.where(
                        low,
                        pltpu.roll(window[:, 0:LANES], HD, 1),
                        pltpu.roll(window[:, LANES:], HD, 1),
                    ),
                    pltpu.roll(window[:, LANES:], HD, 1),
                ],
                axis=1,
            )
        share_out[t] = window[0:REQ]
    sum_experts = [
        push(3, d, share_out.at[lax.rem(tp + d, ntp)], share_in.at[d], on_tp(d))
        for d in range(1, ntp)
    ]

    def scatter(first, near, far, send, last, hops, kind, peer, number_of):
        near[1].wait_recv()
        near[7].wait_recv()
        for copy in far:
            copy.wait_recv()
        heads = [first[d, PG].astype(F32) for d in range(8)]

        def packet(e, out):
            wanted = number_of(e).astype(F32)
            upper = jnp.zeros((PG, TILE, LANES), BF16)
            lower = upper
            for d, head in enumerate(heads):
                mine = jnp.where(head == wanted, 1.0, 0.0).astype(BF16)[None]
                upper = upper + first[d, 0:PG] * mine
                lower = lower + first[d, PG + 1 :] * mine
            out[0:PG] = upper
            out[PG:] = lower

        def send_to(e, sem, src, dst):
            return push(kind, sem, src, dst, peer(e))

        packet(4, send.at[4])
        sent = {
            4: send_to(2, 4, send.at[4, pl.ds(0, PG)], hops.at[2, pl.ds(0, PG)]),
            0: send_to(6, 0, send.at[4, pl.ds(PG, PG)], hops.at[2, pl.ds(PG, PG)]),
        }
        packet(3, send.at[3])
        sent[3] = send_to(1, 3, send.at[3], hops.at[0])
        packet(5, send.at[5])
        sent[5] = send_to(7, 5, send.at[5], hops.at[1])
        for e in (1, 7):
            packet(e, send.at[e])
            sent[e] = send_to(e, e, send.at[e], last.at[e])
        for e in (2, 6):
            packet(e, send.at[e])
        packet(0, last.at[0])
        return sent

    def scatter_on(sent, send, last, hops, kind, peer):
        sent[3].wait_recv()
        sent[4].wait_recv()
        send[2] = send[2] + hops[0]
        send[2, 0:PG] = send[2, 0:PG] + hops[2, 0:PG]
        sent[2] = push(kind, 2, send.at[2], last.at[2], peer(2))
        sent[5].wait_recv()
        sent[0].wait_recv()
        send[6] = send[6] + hops[1]
        send[6, PG:] = send[6, PG:] + hops[2, PG:]
        sent[6] = push(kind, 6, send.at[6], last.at[6], peer(6))

    def number_z(e):
        return lax.rem(z + e, nz) * ny + y

    def number_y(e):
        return z * ny + lax.rem(y + e, ny)

    sent_a = scatter(first_a, near_a, far_a, send_a, last_a, hops_a, 4, on_z, number_z)

    hidden = share_out[tp]
    for d in range(1, ntp):
        sum_experts[d - 1].wait_recv()
        hidden = hidden + share_in[d]
    slot_no = lax.broadcasted_iota(jnp.int32, hidden.shape, 0)
    leaving = jnp.sum(jnp.where(slot_no == leave, hidden, 0.0), axis=0, keepdims=True)
    page_no = lax.shift_right_logical(len_ref[leave], 7)
    line = lax.broadcasted_iota(jnp.int32, (4, LANES), 0)
    row_y[0] = jnp.where(
        line == 0,
        leaving[:, 0:LANES],
        jnp.where(
            line == 1,
            leaving[:, LANES:],
            jnp.where(line == 2, target, page_no).astype(F32),
        ),
    )
    rows_y = [push(6, d, row_y.at[0], row_y.at[d], on_y(d)) for d in range(1, ny)]
    sent_b = scatter(first_b, near_b, far_b, send_b, last_b, hops_b, 5, on_y, number_y)
    scatter_on(sent_a, send_a, last_a, hops_a, 4, on_z)
    scatter_on(sent_b, send_b, last_b, hops_b, 5, on_y)
    for copy in rows_y:
        copy.wait_recv()
    rows_z = []
    for e in range(nz):
        wanted = number_z(e).astype(F32)
        message = jnp.zeros((4, LANES), F32)
        for d in range(ny):
            one = row_y[d]
            message = message + jnp.where(one[2:3, :] == wanted, 1.0, 0.0) * one
        if e == 0:
            row_z[0] = message
        else:
            row_send[e] = message
            rows_z.append(push(7, e, row_send.at[e], row_z.at[e], on_z(e)))
    message = row_z[0]
    for e in range(1, nz):
        rows_z[e - 1].wait_recv()
        message = message + row_z[e]
    moved_row = jnp.concatenate([message[0:1, :], message[1:2, :]], axis=1)
    hidden = jnp.where(slot_no == leave, moved_row, hidden)
    hid_out[...] = hidden[0:REQ, 0:cols].astype(BF16)

    came_page = jnp.broadcast_to(message[3:4, :], (TILE, LANES))
    moved = jnp.zeros((PG, TILE, LANES), BF16)
    for last, sent, p0 in ((last_a, sent_a, 0), (last_b, sent_b, 2)):
        came = last[0]
        for e in (1, 7, 2, 6):
            sent[e].wait_recv()
            came = came + last[e]
        for i in range(2):
            page = came[i * PG : (i + 1) * PG]
            arr_out[p0 + i] = page.reshape(PAGE, LANES)
            mine = jnp.where(came_page == float(p0 + i), 1.0, 0.0).astype(BF16)
            moved = moved + page * mine[None]
    for r in range(REQ):
        kept = jnp.full((TILE, LANES), jnp.where(leave == r, 0.0, 1.0), F32)
        stays = cache[r, lax.shift_right_logical(len_ref[r], 7)].reshape(PG, TILE, LANES)
        page = stays * kept.astype(BF16)[None] + moved * (1.0 - kept).astype(BF16)[None]
        newp_out[r] = page.reshape(PAGE, LANES)

    for copies in (
        near_a.values(),
        near_b.values(),
        far_a,
        far_b,
        sum_heads,
        sum_experts,
        sent_a.values(),
        sent_b.values(),
        rows_y,
        rows_z,
    ):
        for copy in copies:
            copy.wait_send()


def write_out(hid, newp, arr, hid_hbm, newp_hbm, arr_hbm, sem):
    copies = [
        pltpu.make_async_copy(src, dst, sem.at[i])
        for i, (src, dst) in enumerate(((hid, hid_hbm), (newp, newp_hbm), (arr, arr_hbm)))
    ]
    for copy in copies:
        copy.start()
    for copy in copies:
        copy.wait()


def local(
    nz,
    ny,
    ntp,
    kv_pool,
    page_table,
    req_lengths,
    leave_slot,
    target_rep,
    qkv_new,
    residual_in,
    expert_ids,
    gate_weights,
    norm_gain,
    out_proj,
    expert_in,
    expert_down,
):
    width = residual_in.shape[1]
    cols = width // ntp
    most = max(nz, ny, ntp)
    vmem = pl.BlockSpec(memory_space=pltpu.VMEM)
    hbm = pl.BlockSpec(memory_space=pltpu.HBM)
    shapes = ((REQ, cols), (REQ, PAGE, LANES), (MAXP, PAGE, LANES))
    results = pl.pallas_call(
        functools.partial(kernel, nz, ny, ntp),
        out_shape=tuple(pltpu.VMEM(s, BF16) for s in shapes),
        in_specs=[hbm] * 13,
        out_specs=(vmem, vmem, vmem),
        scratch_shapes=[
            pltpu.SMEM(page_table.shape, jnp.int32),
            pltpu.SMEM(req_lengths.shape, jnp.int32),
            pltpu.SMEM(leave_slot.shape, jnp.int32),
            pltpu.SMEM(target_rep.shape, jnp.int32),
            pltpu.VMEM(qkv_new.shape, BF16),
            pltpu.VMEM(residual_in.shape, BF16),
            pltpu.VMEM(expert_ids.shape, jnp.int32),
            pltpu.VMEM(gate_weights.shape, BF16),
            pltpu.VMEM(norm_gain.shape, F32),
            pltpu.VMEM(kv_pool.shape, BF16),
            pltpu.VMEM(out_proj.shape, BF16),
            pltpu.VMEM(expert_in.shape[1:], BF16),
            pltpu.VMEM(expert_down.shape[1:], BF16),
            pltpu.VMEM((8, 3 * LANES), F32),
            pltpu.VMEM((8, LANES), F32),
            pltpu.VMEM((REQ, MAXP, PAGE, LANES), BF16),
            pltpu.VMEM((ny, 2 * PG + 1, TILE, LANES), BF16),
            pltpu.VMEM((nz, 2 * PG + 1, TILE, LANES), BF16),
            pltpu.VMEM((nz, 2 * PG, TILE, LANES), BF16),
            pltpu.VMEM((ny, 2 * PG, TILE, LANES), BF16),
            pltpu.VMEM((nz, 2 * PG, TILE, LANES), BF16),
            pltpu.VMEM((ny, 2 * PG, TILE, LANES), BF16),
            pltpu.VMEM((3, 2 * PG, TILE, LANES), BF16),
            pltpu.VMEM((3, 2 * PG, TILE, LANES), BF16),
            pltpu.VMEM((ntp, REQ, width), BF16),
            pltpu.VMEM((8, width), F32),
            pltpu.VMEM((ntp, REQ, 2 * LANES), F32),
            pltpu.VMEM((ntp, REQ, 2 * LANES), F32),
            pltpu.VMEM((ny, 4, LANES), F32),
            pltpu.VMEM((nz, 4, LANES), F32),
            pltpu.VMEM((nz, 4, LANES), F32),
            pltpu.SemaphoreType.DMA((13,)),
            pltpu.SemaphoreType.DMA((8, most)),
            pltpu.SemaphoreType.DMA((8, most)),
            pltpu.SemaphoreType.REGULAR,
        ],
        compiler_params=pltpu.CompilerParams(
            collective_id=0, has_side_effects=True, vmem_limit_bytes=60 << 20
        ),
    )(
        page_table,
        req_lengths,
        leave_slot,
        target_rep,
        qkv_new,
        residual_in,
        expert_ids,
        gate_weights,
        norm_gain,
        kv_pool,
        out_proj,
        expert_in,
        expert_down,
    )
    return pl.pallas_call(
        write_out,
        out_shape=tuple(jax.ShapeDtypeStruct(s, BF16) for s in shapes),
        in_specs=[vmem] * 3,
        out_specs=[hbm] * 3,
        scratch_shapes=[pltpu.SemaphoreType.DMA((3,))],
        compiler_params=pltpu.CompilerParams(vmem_limit_bytes=1 << 20),
    )(*results)


def solution(mesh):
    nrep, ntp = mesh.shape["rep"], mesh.shape["tp"]
    ny = math.isqrt(nrep)
    return jax.shard_map(
        functools.partial(local, nrep // ny, ny, ntp),
        mesh=mesh,
        in_specs=(
            P("rep", None, "tp"),
            P("rep", None),
            P("rep"),
            P("rep"),
            P("rep"),
            P("rep", "tp"),
            P("rep", None),
            P("rep", None),
            P("rep", None),
            P(),
            P("tp", None),
            P("tp", None, None),
            P("tp", None, None),
        ),
        out_specs=(P("rep", "tp"), P("rep", None, "tp"), P("rep", None, "tp")),
        check_vma=False,
    )
```

```python
import functools
import math

import jax
import jax.numpy as jnp
from jax import lax
from jax.experimental import pallas as pl
from jax.experimental.pallas import tpu as pltpu
from jax.sharding import PartitionSpec as P

HD = 64
PAGE = 128
MAXP = 4
REQ = 4
GROUP = 3
LANES = 128
TILE = 16
PG = PAGE // TILE
F32 = jnp.float32
BF16 = jnp.bfloat16
MESH = pl.DeviceIdType.MESH


def dot(a, b):
    return jnp.dot(a, b, preferred_element_type=F32)


def kernel(
    nz,
    ny,
    ntp,
    pt_hbm,
    len_hbm,
    leave_hbm,
    target_hbm,
    qkv_hbm,
    res_hbm,
    ids_hbm,
    gate_hbm,
    gain_hbm,
    pool_hbm,
    wo_hbm,
    win_hbm,
    wd_hbm,
    hid_out,
    newp_out,
    arr_out,
    pt_ref,
    len_ref,
    leave_ref,
    target_ref,
    qkv_ref,
    res_ref,
    ids_ref,
    gate_ref,
    gain_ref,
    pool,
    wo,
    win,
    wd,
    qs,
    new_kv,
    cache,
    first_a,
    first_b,
    send_a,
    send_b,
    last_a,
    last_b,
    hops_a,
    hops_b,
    parts,
    stream8,
    share_out,
    share_in,
    row_y,
    row_send,
    row_z,
    load_sem,
    send_sem,
    recv_sem,
    ready_sem,
):
    rep = lax.axis_index("rep")
    tp = lax.axis_index("tp")
    z = lax.div(rep, ny)
    y = lax.rem(rep, ny)

    ring_y = [{"rep": z * ny + lax.rem(y + step, ny)} for step in range(ny)]
    ring_z = [{"rep": lax.rem(z + step, nz) * ny + y} for step in range(nz)]
    ring_tp = [{"tp": lax.rem(tp + step, ntp)} for step in range(ntp)]
    on_y, on_z, on_tp = ring_y.__getitem__, ring_z.__getitem__, ring_tp.__getitem__

    pairs = (
        (pt_hbm, pt_ref),
        (len_hbm, len_ref),
        (leave_hbm, leave_ref),
        (target_hbm, target_ref),
        (qkv_hbm, qkv_ref),
        (pool_hbm, pool),
        (wo_hbm, wo),
        (res_hbm, res_ref),
        (ids_hbm, ids_ref),
        (gate_hbm, gate_ref),
        (gain_hbm, gain_ref),
        (win_hbm.at[0], win),
        (wd_hbm.at[0], wd),
    )
    loads = [
        pltpu.make_async_copy(src, dst, load_sem.at[i]) for i, (src, dst) in enumerate(pairs)
    ]
    for copy in loads[0:6]:
        copy.start()

    is_late = rep * ntp + tp == 0
    near_y = (1, 2, ny - 2, ny - 1)
    near_z = (1, 2, nz - 2, nz - 1)

    def beside(place, steps):
        hits = [place == step for step in steps]
        return functools.reduce(jnp.logical_or, hits)

    late_y = jnp.logical_and(z * ntp + tp == 0, beside(y, near_y))
    late_z = jnp.logical_and(y * ntp + tp == 0, beside(z, near_z))
    late_tp = jnp.logical_and(rep == 0, tp != 0)
    late_peer = jnp.logical_or(jnp.logical_or(late_y, late_z), late_tp)
    everyone = [
        peer(step)
        for peer, steps in ((on_y, near_y), (on_z, near_z), (on_tp, range(1, ntp)))
        for step in steps
    ]
    barrier = pltpu.get_barrier_semaphore()

    @pl.when(jnp.logical_not(is_late))
    def _():
        for device in everyone:
            pl.semaphore_signal(barrier, inc=1, device_id=device, device_id_type=MESH)

    @pl.when(is_late)
    def _():
        pl.semaphore_wait(barrier, len(everyone))
        for device in everyone:
            pl.semaphore_signal(ready_sem, inc=1, device_id=device, device_id_type=MESH)

    def push(kind, sem, src, dst, device, start=None):
        copy = pltpu.make_async_remote_copy(
            src_ref=src,
            dst_ref=dst,
            send_sem=send_sem.at[kind, sem],
            recv_sem=recv_sem.at[kind, sem],
            device_id=device,
            device_id_type=MESH,
        )
        if start is None:
            copy.start()
        else:
            pl.when(start)(copy.start)
        return copy

    for copy in loads[0:5]:
        copy.wait()
    leave = leave_ref[0]
    target = target_ref[0]
    low = lax.broadcasted_iota(jnp.int32, (8, LANES), 1) < HD
    qs[...] = jnp.zeros_like(qs)
    qs[0:REQ, 0 : (GROUP + 2) * HD] = qkv_ref[...].astype(F32)
    qkv_a, qkv_b, qkv_c = qs[:, 0:128], qs[:, 128:256], qs[:, 256:384]
    zero8 = jnp.zeros((8, LANES), F32)
    queries = jnp.concatenate(
        [
            jnp.where(low, qkv_a, zero8),
            jnp.where(low, pltpu.roll(qkv_a, HD, 1), zero8),
            jnp.where(low, qkv_b, zero8),
        ],
        axis=0,
    ).astype(BF16)
    fresh = jnp.where(low, pltpu.roll(qkv_b, HD, 1), pltpu.roll(qkv_c, HD, 1))

    loads[5].wait()
    for copy in loads[6:]:
        copy.start()
    new_kv[...] = fresh
    row_in_page = lax.broadcasted_iota(jnp.int32, (PAGE, LANES), 0)

    def with_token(r, p):
        at_token = row_in_page == len_ref[r] - p * PAGE
        page = pool[pt_ref[r, p]].astype(F32)
        return jnp.where(at_token, new_kv[pl.ds(r, 1), :], page).astype(BF16)

    header = jnp.full((TILE, LANES), target, jnp.int32).astype(F32).astype(BF16)
    for buf, p0 in ((first_a, 0), (first_b, 2)):
        buf[0, 0:PG] = with_token(leave, p0).reshape(PG, TILE, LANES)
        buf[0, PG] = header
        buf[0, PG + 1 :] = with_token(leave, p0 + 1).reshape(PG, TILE, LANES)

    @pl.when(jnp.logical_not(is_late))
    def _():
        pl.semaphore_wait(barrier, len(everyone) - late_peer.astype(jnp.int32))

    def to_late(flag, place, step, count):
        return jnp.logical_and(flag, place + step == count)

    def spread(kind, first, peer, flag, place, count):
        near = {}
        for d in (2, count - 2, 1, count - 1):
            late = to_late(flag, place, d, count)
            near[d] = push(kind, d, first.at[0], first.at[d], peer(d), jnp.logical_not(late))
        return near

    def spread_late(near, flag, place, count):
        for d, copy in near.items():
            pl.when(to_late(flag, place, d, count))(copy.start)

    def pass_on(kind, first, peer, near):
        upper, lower = pl.ds(0, PG + 1), pl.ds(PG + 1, PG)
        near[2].wait_recv()
        far = [
            push(kind, 4, first.at[2, upper], first.at[4, upper], peer(2)),
            push(kind, 3, first.at[2], first.at[3], peer(1)),
        ]
        near[6].wait_recv()
        far += [
            push(kind, 0, first.at[6, lower], first.at[4, lower], peer(6)),
            push(kind, 5, first.at[6], first.at[5], peer(7)),
        ]
        return far

    near_a = spread(0, first_a, on_y, late_y, y, ny)
    near_b = spread(1, first_b, on_z, late_z, z, nz)

    for r in range(REQ):
        for p in range(MAXP):
            cache[r, p] = with_token(r, p)

    span = MAXP * PAGE
    row_req = lax.broadcasted_iota(jnp.int32, (GROUP * 8, span), 0) & 7
    position = lax.broadcasted_iota(jnp.int32, (GROUP * 8, span), 1)
    scores = jnp.zeros((GROUP * 8, span), F32)
    limit = jnp.zeros((GROUP * 8, span), jnp.int32)
    for r in range(REQ):
        rows = cache[r].reshape(span, LANES)
        one = lax.dot_general(
            queries, rows, (((1,), (1,)), ((), ())), preferred_element_type=F32
        )
        scores = jnp.where(row_req == r, one, scores)
        limit = jnp.where(row_req == r, len_ref[r], limit)
    scores = jnp.where(position <= limit, scores * (1.0 / math.sqrt(HD)), -jnp.inf)
    weights = jnp.exp(scores - jnp.max(scores, axis=1, keepdims=True))
    probs = weights / jnp.sum(weights, axis=1, keepdims=True)
    attn = jnp.zeros((GROUP * 8, LANES), F32)
    for r in range(REQ):
        rows = cache[r].reshape(span, LANES)
        attn = attn + dot(jnp.where(row_req == r, probs, 0.0).astype(BF16), rows)
    heads01 = jnp.where(low, pltpu.roll(attn[0:8], HD, 1), attn[8:16]).astype(BF16)
    head2 = pltpu.roll(attn[16:24], HD, 1)[:, 0:HD].astype(BF16)
    loads[6].wait()
    part = dot(heads01, wo[0:LANES, :]) + dot(head2, wo[LANES : LANES + HD, :])
    parts[0] = part[0:REQ]

    @pl.when(late_peer)
    def _():
        pl.semaphore_wait(ready_sem, 1)

    spread_late(near_a, late_y, y, ny)
    spread_late(near_b, late_z, z, nz)
    sum_heads = [push(2, d, parts.at[0], parts.at[d], on_tp(d)) for d in range(1, ntp)]

    far_a = pass_on(0, first_a, on_y, near_a)
    far_b = pass_on(1, first_b, on_z, near_b)

    for copy in loads[7:11]:
        copy.wait()
    share = jnp.sum(
        jnp.where(ids_ref[...] == tp, gate_ref[...].astype(F32), 0.0), axis=1, keepdims=True
    )
    total = res_ref[...].astype(F32) + part[0:REQ]
    for d in range(1, ntp):
        sum_heads[d - 1].wait_recv()
        total = total + parts[d]
    stream8[...] = jnp.zeros_like(stream8)
    stream8[0:REQ, :] = total
    stream = stream8[...]
    mean_sq = jnp.mean(stream * stream, axis=1, keepdims=True)
    normed = (stream * lax.rsqrt(mean_sq + 1e-05) * gain_ref[...][None, :]).astype(BF16)
    loads[11].wait()
    up = dot(normed, win[...])
    half = up.shape[1] // 2
    gate, lift = up[:, 0:half], up[:, half:]
    acted = (gate * (1.0 / (1.0 + jnp.exp(-gate))) * lift).astype(BF16)
    loads[12].wait()
    down = dot(acted, wd[...])
    stream8[0:REQ, :] = down[0:REQ] * share + jnp.where(tp == 0, 1.0, 0.0) * total
    cols = stream8.shape[1] // ntp
    for t in range(ntp):
        start = t * cols // LANES * LANES
        window = stream8[:, start : start + 2 * LANES]
        if t * cols != start:
            window = jnp.concatenate(
                [
                    jnp.where(
                        low,
                        pltpu.roll(window[:, 0:LANES], HD, 1),
                        pltpu.roll(window[:, LANES:], HD, 1),
                    ),
                    pltpu.roll(window[:, LANES:], HD, 1),
                ],
                axis=1,
            )
        share_out[t] = window[0:REQ]
    sum_experts = [
        push(3, d, share_out.at[lax.rem(tp + d, ntp)], share_in.at[d], on_tp(d))
        for d in range(1, ntp)
    ]

    def scatter(first, near, far, send, last, hops, kind, peer, number_of):
        near[1].wait_recv()
        near[7].wait_recv()
        for copy in far:
            copy.wait_recv()
        heads = [first[d, PG].astype(F32) for d in range(8)]

        def packet(e, out):
            wanted = number_of(e).astype(F32)
            upper = jnp.zeros((PG, TILE, LANES), BF16)
            lower = upper
            for d, head in enumerate(heads):
                mine = jnp.where(head == wanted, 1.0, 0.0).astype(BF16)[None]
                upper = upper + first[d, 0:PG] * mine
                lower = lower + first[d, PG + 1 :] * mine
            out[0:PG] = upper
            out[PG:] = lower

        def send_to(e, sem, src, dst):
            return push(kind, sem, src, dst, peer(e))

        packet(4, send.at[4])
        sent = {
            4: send_to(2, 4, send.at[4, pl.ds(0, PG)], hops.at[2, pl.ds(0, PG)]),
            0: send_to(6, 0, send.at[4, pl.ds(PG, PG)], hops.at[2, pl.ds(PG, PG)]),
        }
        packet(3, send.at[3])
        sent[3] = send_to(1, 3, send.at[3], hops.at[0])
        packet(5, send.at[5])
        sent[5] = send_to(7, 5, send.at[5], hops.at[1])
        for e in (1, 7):
            packet(e, send.at[e])
            sent[e] = send_to(e, e, send.at[e], last.at[e])
        def rest():
            for e in (2, 6):
                packet(e, send.at[e])
            packet(0, last.at[0])

        return sent, rest

    def scatter_on(sent, send, last, hops, kind, peer):
        sent[3].wait_recv()
        sent[4].wait_recv()
        send[2] = send[2] + hops[0]
        send[2, 0:PG] = send[2, 0:PG] + hops[2, 0:PG]
        sent[2] = push(kind, 2, send.at[2], last.at[2], peer(2))
        sent[5].wait_recv()
        sent[0].wait_recv()
        send[6] = send[6] + hops[1]
        send[6, PG:] = send[6, PG:] + hops[2, PG:]
        sent[6] = push(kind, 6, send.at[6], last.at[6], peer(6))

    def number_z(e):
        return ring_z[e]["rep"]

    def number_y(e):
        return ring_y[e]["rep"]

    sent_a, rest_a = scatter(first_a, near_a, far_a, send_a, last_a, hops_a, 4, on_z, number_z)

    hidden = share_out[tp]
    for d in range(1, ntp):
        sum_experts[d - 1].wait_recv()
        hidden = hidden + share_in[d]
    slot_no = lax.broadcasted_iota(jnp.int32, hidden.shape, 0)
    leaving = jnp.sum(jnp.where(slot_no == leave, hidden, 0.0), axis=0, keepdims=True)
    page_no = lax.shift_right_logical(len_ref[leave], 7)
    line = lax.broadcasted_iota(jnp.int32, (4, LANES), 0)
    row_y[0] = jnp.where(
        line == 0,
        leaving[:, 0:LANES],
        jnp.where(
            line == 1,
            leaving[:, LANES:],
            jnp.where(line == 2, target, page_no).astype(F32),
        ),
    )
    rows_y = [push(6, d, row_y.at[0], row_y.at[d], on_y(d)) for d in range(1, ny)]
    sent_b, rest_b = scatter(first_b, near_b, far_b, send_b, last_b, hops_b, 5, on_y, number_y)
    rest_a()
    rest_b()
    for copy in rows_y:
        copy.wait_recv()
    rows_z = []
    for e in range(nz):
        wanted = number_z(e).astype(F32)
        message = jnp.zeros((4, LANES), F32)
        for d in range(ny):
            one = row_y[d]
            message = message + jnp.where(one[2:3, :] == wanted, 1.0, 0.0) * one
        if e == 0:
            row_z[0] = message
        else:
            row_send[e] = message
            rows_z.append(push(7, e, row_send.at[e], row_z.at[e], on_z(e)))
    scatter_on(sent_a, send_a, last_a, hops_a, 4, on_z)
    scatter_on(sent_b, send_b, last_b, hops_b, 5, on_y)
    message = row_z[0]
    for e in range(1, nz):
        rows_z[e - 1].wait_recv()
        message = message + row_z[e]
    moved_row = jnp.concatenate([message[0:1, :], message[1:2, :]], axis=1)
    hidden = jnp.where(slot_no == leave, moved_row, hidden)
    hid_out[...] = hidden[0:REQ, 0:cols].astype(BF16)

    came_page = jnp.broadcast_to(message[3:4, :], (TILE, LANES))
    moved = jnp.zeros((PG, TILE, LANES), BF16)
    for last, sent, p0 in ((last_a, sent_a, 0), (last_b, sent_b, 2)):
        came = last[0]
        for e in (1, 7, 2, 6):
            sent[e].wait_recv()
            came = came + last[e]
        for i in range(2):
            page = came[i * PG : (i + 1) * PG]
            arr_out[p0 + i] = page.reshape(PAGE, LANES)
            mine = jnp.where(came_page == float(p0 + i), 1.0, 0.0).astype(BF16)
            moved = moved + page * mine[None]
    for r in range(REQ):
        kept = jnp.full((TILE, LANES), jnp.where(leave == r, 0.0, 1.0), F32)
        stays = cache[r, lax.shift_right_logical(len_ref[r], 7)].reshape(PG, TILE, LANES)
        page = stays * kept.astype(BF16)[None] + moved * (1.0 - kept).astype(BF16)[None]
        newp_out[r] = page.reshape(PAGE, LANES)

    for copies in (
        near_a.values(),
        near_b.values(),
        far_a,
        far_b,
        sum_heads,
        sum_experts,
        sent_a.values(),
        sent_b.values(),
        rows_y,
        rows_z,
    ):
        for copy in copies:
            copy.wait_send()


def write_out(hid, newp, arr, hid_hbm, newp_hbm, arr_hbm, sem):
    copies = [
        pltpu.make_async_copy(src, dst, sem.at[i])
        for i, (src, dst) in enumerate(((hid, hid_hbm), (newp, newp_hbm), (arr, arr_hbm)))
    ]
    for copy in copies:
        copy.start()
    for copy in copies:
        copy.wait()


def local(
    nz,
    ny,
    ntp,
    kv_pool,
    page_table,
    req_lengths,
    leave_slot,
    target_rep,
    qkv_new,
    residual_in,
    expert_ids,
    gate_weights,
    norm_gain,
    out_proj,
    expert_in,
    expert_down,
):
    width = residual_in.shape[1]
    cols = width // ntp
    most = max(nz, ny, ntp)
    vmem = pl.BlockSpec(memory_space=pltpu.VMEM)
    hbm = pl.BlockSpec(memory_space=pltpu.HBM)
    shapes = ((REQ, cols), (REQ, PAGE, LANES), (MAXP, PAGE, LANES))
    results = pl.pallas_call(
        functools.partial(kernel, nz, ny, ntp),
        out_shape=tuple(pltpu.VMEM(s, BF16) for s in shapes),
        in_specs=[hbm] * 13,
        out_specs=(vmem, vmem, vmem),
        scratch_shapes=[
            pltpu.SMEM(page_table.shape, jnp.int32),
            pltpu.SMEM(req_lengths.shape, jnp.int32),
            pltpu.SMEM(leave_slot.shape, jnp.int32),
            pltpu.SMEM(target_rep.shape, jnp.int32),
            pltpu.VMEM(qkv_new.shape, BF16),
            pltpu.VMEM(residual_in.shape, BF16),
            pltpu.VMEM(expert_ids.shape, jnp.int32),
            pltpu.VMEM(gate_weights.shape, BF16),
            pltpu.VMEM(norm_gain.shape, F32),
            pltpu.VMEM(kv_pool.shape, BF16),
            pltpu.VMEM(out_proj.shape, BF16),
            pltpu.VMEM(expert_in.shape[1:], BF16),
            pltpu.VMEM(expert_down.shape[1:], BF16),
            pltpu.VMEM((8, 3 * LANES), F32),
            pltpu.VMEM((8, LANES), F32),
            pltpu.VMEM((REQ, MAXP, PAGE, LANES), BF16),
            pltpu.VMEM((ny, 2 * PG + 1, TILE, LANES), BF16),
            pltpu.VMEM((nz, 2 * PG + 1, TILE, LANES), BF16),
            pltpu.VMEM((nz, 2 * PG, TILE, LANES), BF16),
            pltpu.VMEM((ny, 2 * PG, TILE, LANES), BF16),
            pltpu.VMEM((nz, 2 * PG, TILE, LANES), BF16),
            pltpu.VMEM((ny, 2 * PG, TILE, LANES), BF16),
            pltpu.VMEM((3, 2 * PG, TILE, LANES), BF16),
            pltpu.VMEM((3, 2 * PG, TILE, LANES), BF16),
            pltpu.VMEM((ntp, REQ, width), F32),
            pltpu.VMEM((8, width), F32),
            pltpu.VMEM((ntp, REQ, 2 * LANES), F32),
            pltpu.VMEM((ntp, REQ, 2 * LANES), F32),
            pltpu.VMEM((ny, 4, LANES), F32),
            pltpu.VMEM((nz, 4, LANES), F32),
            pltpu.VMEM((nz, 4, LANES), F32),
            pltpu.SemaphoreType.DMA((13,)),
            pltpu.SemaphoreType.DMA((8, most)),
            pltpu.SemaphoreType.DMA((8, most)),
            pltpu.SemaphoreType.REGULAR,
        ],
        compiler_params=pltpu.CompilerParams(
            collective_id=0, has_side_effects=True, vmem_limit_bytes=60 << 20
        ),
    )(
        page_table,
        req_lengths,
        leave_slot,
        target_rep,
        qkv_new,
        residual_in,
        expert_ids,
        gate_weights,
        norm_gain,
        kv_pool,
        out_proj,
        expert_in,
        expert_down,
    )
    return pl.pallas_call(
        write_out,
        out_shape=tuple(jax.ShapeDtypeStruct(s, BF16) for s in shapes),
        in_specs=[vmem] * 3,
        out_specs=[hbm] * 3,
        scratch_shapes=[pltpu.SemaphoreType.DMA((3,))],
        compiler_params=pltpu.CompilerParams(vmem_limit_bytes=1 << 20),
    )(*results)


def solution(mesh):
    nrep, ntp = mesh.shape["rep"], mesh.shape["tp"]
    ny = math.isqrt(nrep)
    return jax.shard_map(
        functools.partial(local, nrep // ny, ny, ntp),
        mesh=mesh,
        in_specs=(
            P("rep", None, "tp"),
            P("rep", None),
            P("rep"),
            P("rep"),
            P("rep"),
            P("rep", "tp"),
            P("rep", None),
            P("rep", None),
            P("rep", None),
            P(),
            P("tp", None),
            P("tp", None, None),
            P("tp", None, None),
        ),
        out_specs=(P("rep", "tp"), P("rep", None, "tp"), P("rep", None, "tp")),
        check_vma=False,
    )
```

```python
import functools
import math

import jax
import jax.numpy as jnp
from jax import lax
from jax.experimental import pallas as pl
from jax.experimental.pallas import tpu as pltpu
from jax.sharding import PartitionSpec as P

HD = 64
PAGE = 128
MAXP = 4
REQ = 4
GROUP = 3
LANES = 128
TILE = 16
PG = PAGE // TILE
F32 = jnp.float32
BF16 = jnp.bfloat16
MESH = pl.DeviceIdType.MESH


def dot(a, b):
    return jnp.dot(a, b, preferred_element_type=F32)


def kernel(
    nz,
    ny,
    ntp,
    pt_hbm,
    len_hbm,
    leave_hbm,
    target_hbm,
    qkv_hbm,
    res_hbm,
    ids_hbm,
    gate_hbm,
    gain_hbm,
    pool_hbm,
    wo_hbm,
    win_hbm,
    wd_hbm,
    hid_out,
    newp_out,
    arr_out,
    pt_ref,
    len_ref,
    leave_ref,
    target_ref,
    qkv_ref,
    res_ref,
    ids_ref,
    gate_ref,
    gain_ref,
    pool,
    wo,
    win,
    wd,
    qs,
    new_kv,
    cache,
    first_a,
    first_b,
    send_a,
    send_b,
    last_a,
    last_b,
    hops_a,
    hops_b,
    parts,
    stream8,
    share_out,
    share_in,
    row_y,
    row_send,
    row_z,
    load_sem,
    send_sem,
    recv_sem,
    ready_sem,
):
    rep = lax.axis_index("rep")
    tp = lax.axis_index("tp")
    z = lax.div(rep, ny)
    y = lax.rem(rep, ny)

    def on_y(step):
        return {"rep": z * ny + lax.rem(y + step, ny)}

    def on_z(step):
        return {"rep": lax.rem(z + step, nz) * ny + y}

    def on_tp(step):
        return {"tp": lax.rem(tp + step, ntp)}

    pairs = (
        (pt_hbm, pt_ref),
        (len_hbm, len_ref),
        (leave_hbm, leave_ref),
        (target_hbm, target_ref),
        (qkv_hbm, qkv_ref),
        (pool_hbm, pool),
        (wo_hbm, wo),
        (res_hbm, res_ref),
        (ids_hbm, ids_ref),
        (gate_hbm, gate_ref),
        (gain_hbm, gain_ref),
        (win_hbm.at[0], win),
        (wd_hbm.at[0], wd),
    )
    loads = [
        pltpu.make_async_copy(src, dst, load_sem.at[i]) for i, (src, dst) in enumerate(pairs)
    ]
    for copy in loads[0:6]:
        copy.start()

    is_late = rep * ntp + tp == 0
    near_y = (1, 2, ny - 2, ny - 1)
    near_z = (1, 2, nz - 2, nz - 1)

    def beside(place, steps):
        hits = [place == step for step in steps]
        return functools.reduce(jnp.logical_or, hits)

    late_y = jnp.logical_and(z * ntp + tp == 0, beside(y, near_y))
    late_z = jnp.logical_and(y * ntp + tp == 0, beside(z, near_z))
    late_tp = jnp.logical_and(rep == 0, tp != 0)
    late_peer = jnp.logical_or(jnp.logical_or(late_y, late_z), late_tp)
    everyone = [
        peer(step)
        for peer, steps in ((on_y, near_y), (on_z, near_z), (on_tp, range(1, ntp)))
        for step in steps
    ]
    barrier = pltpu.get_barrier_semaphore()

    @pl.when(jnp.logical_not(is_late))
    def _():
        for device in everyone:
            pl.semaphore_signal(barrier, inc=1, device_id=device, device_id_type=MESH)

    @pl.when(is_late)
    def _():
        pl.semaphore_wait(barrier, len(everyone))
        for device in everyone:
            pl.semaphore_signal(ready_sem, inc=1, device_id=device, device_id_type=MESH)

    def push(kind, sem, src, dst, device, start=None):
        copy = pltpu.make_async_remote_copy(
            src_ref=src,
            dst_ref=dst,
            send_sem=send_sem.at[kind, sem],
            recv_sem=recv_sem.at[kind, sem],
            device_id=device,
            device_id_type=MESH,
        )
        if start is None:
            copy.start()
        else:
            pl.when(start)(copy.start)
        return copy

    for copy in loads[0:5]:
        copy.wait()
    leave = leave_ref[0]
    target = target_ref[0]
    low = lax.broadcasted_iota(jnp.int32, (8, LANES), 1) < HD
    qs[...] = jnp.zeros_like(qs)
    qs[0:REQ, 0 : (GROUP + 2) * HD] = qkv_ref[...].astype(F32)
    qkv_a, qkv_b, qkv_c = qs[:, 0:128], qs[:, 128:256], qs[:, 256:384]
    zero8 = jnp.zeros((8, LANES), F32)
    queries = jnp.concatenate(
        [
            jnp.where(low, qkv_a, zero8),
            jnp.where(low, pltpu.roll(qkv_a, HD, 1), zero8),
            jnp.where(low, qkv_b, zero8),
        ],
        axis=0,
    ).astype(BF16)
    fresh = jnp.where(low, pltpu.roll(qkv_b, HD, 1), pltpu.roll(qkv_c, HD, 1))

    loads[5].wait()
    for copy in loads[6:]:
        copy.start()
    new_kv[...] = fresh
    row_in_page = lax.broadcasted_iota(jnp.int32, (PAGE, LANES), 0)

    def with_token(r, p):
        at_token = row_in_page == len_ref[r] - p * PAGE
        page = pool[pt_ref[r, p]].astype(F32)
        return jnp.where(at_token, new_kv[pl.ds(r, 1), :], page).astype(BF16)

    header = jnp.full((TILE, LANES), target, jnp.int32).astype(F32).astype(BF16)
    for c in range(2):
        for buf, p0 in ((first_a, 0), (first_b, 2)):
            buf[c, 0, 0:PG] = with_token(leave, p0 + c).reshape(PG, TILE, LANES)
            if c == 0:
                buf[0, 0, PG] = header

    @pl.when(jnp.logical_not(is_late))
    def _():
        pl.semaphore_wait(barrier, len(everyone) - late_peer.astype(jnp.int32))

    def to_late(flag, place, step, count):
        return jnp.logical_and(flag, place + step == count)

    def slot(first, c, d):
        return first.at[c, d] if c == 0 else first.at[c, d, pl.ds(0, PG)]

    def spread(kind, first, c, peer, flag, place, count):
        near = {}
        for d in (2, 6, 1, 7):
            late = to_late(flag, place, d, count)
            near[d] = push(
                kind, d, slot(first, c, 0), slot(first, c, d), peer(d), jnp.logical_not(late)
            )
        return near

    def spread_late(near, flag, place, count):
        for d, copy in near.items():
            pl.when(to_late(flag, place, d, count))(copy.start)

    def pass_on(kind, first, c, peer, near):
        far = []
        for held, d, step in ((2, 3, 1), (6, 5, 7)):
            near[held].wait_recv()
            if held == (2, 6)[c]:
                far.append(push(kind, 4, slot(first, c, held), slot(first, c, 4), peer(held)))
            far.append(push(kind, d, slot(first, c, held), slot(first, c, d), peer(step)))
        return far

    near_a, near_b = [], []
    for c in range(2):
        near_a.append(spread(c, first_a, c, on_y, late_y, y, ny))
        near_b.append(spread(2 + c, first_b, c, on_z, late_z, z, nz))

    for r in range(REQ):
        for p in range(MAXP):
            cache[r, p] = with_token(r, p)

    span = MAXP * PAGE
    row_req = lax.broadcasted_iota(jnp.int32, (GROUP * 8, span), 0) & 7
    position = lax.broadcasted_iota(jnp.int32, (GROUP * 8, span), 1)
    scores = jnp.zeros((GROUP * 8, span), F32)
    limit = jnp.zeros((GROUP * 8, span), jnp.int32)
    for r in range(REQ):
        rows = cache[r].reshape(span, LANES)
        one = lax.dot_general(
            queries, rows, (((1,), (1,)), ((), ())), preferred_element_type=F32
        )
        scores = jnp.where(row_req == r, one, scores)
        limit = jnp.where(row_req == r, len_ref[r], limit)
    scores = jnp.where(position <= limit, scores * (1.0 / math.sqrt(HD)), -jnp.inf)
    weights = jnp.exp(scores - jnp.max(scores, axis=1, keepdims=True))
    probs = weights / jnp.sum(weights, axis=1, keepdims=True)
    attn = jnp.zeros((GROUP * 8, LANES), F32)
    for r in range(REQ):
        rows = cache[r].reshape(span, LANES)
        attn = attn + dot(jnp.where(row_req == r, probs, 0.0).astype(BF16), rows)
    heads01 = jnp.where(low, pltpu.roll(attn[0:8], HD, 1), attn[8:16]).astype(BF16)
    head2 = pltpu.roll(attn[16:24], HD, 1)[:, 0:HD].astype(BF16)
    loads[6].wait()
    part = dot(heads01, wo[0:LANES, :]) + dot(head2, wo[LANES : LANES + HD, :])
    parts[0] = part[0:REQ]

    @pl.when(late_peer)
    def _():
        pl.semaphore_wait(ready_sem, 1)

    for c in range(2):
        spread_late(near_a[c], late_y, y, ny)
        spread_late(near_b[c], late_z, z, nz)
    sum_heads = [push(8, d, parts.at[0], parts.at[d], on_tp(d)) for d in range(1, ntp)]

    far_a, far_b = [], []
    for c in range(2):
        far_a.append(pass_on(c, first_a, c, on_y, near_a[c]))
        far_b.append(pass_on(2 + c, first_b, c, on_z, near_b[c]))

    for copy in loads[7:11]:
        copy.wait()
    share = jnp.sum(
        jnp.where(ids_ref[...] == tp, gate_ref[...].astype(F32), 0.0), axis=1, keepdims=True
    )
    total = res_ref[...].astype(F32) + part[0:REQ]
    for d in range(1, ntp):
        sum_heads[d - 1].wait_recv()
        total = total + parts[d]
    stream8[...] = jnp.zeros_like(stream8)
    stream8[0:REQ, :] = total
    stream = stream8[...]
    mean_sq = jnp.mean(stream * stream, axis=1, keepdims=True)
    normed = (stream * lax.rsqrt(mean_sq + 1e-05) * gain_ref[...][None, :]).astype(BF16)
    loads[11].wait()
    up = dot(normed, win[...])
    half = up.shape[1] // 2
    gate, lift = up[:, 0:half], up[:, half:]
    acted = (gate * (1.0 / (1.0 + jnp.exp(-gate))) * lift).astype(BF16)
    loads[12].wait()
    down = dot(acted, wd[...])
    stream8[0:REQ, :] = down[0:REQ] * share + jnp.where(tp == 0, 1.0, 0.0) * total
    cols = stream8.shape[1] // ntp
    for t in range(ntp):
        start = t * cols // LANES * LANES
        window = stream8[:, start : start + 2 * LANES]
        if t * cols != start:
            window = jnp.concatenate(
                [
                    jnp.where(
                        low,
                        pltpu.roll(window[:, 0:LANES], HD, 1),
                        pltpu.roll(window[:, LANES:], HD, 1),
                    ),
                    pltpu.roll(window[:, LANES:], HD, 1),
                ],
                axis=1,
            )
        share_out[t] = window[0:REQ]
    sum_experts = [
        push(9, d, share_out.at[lax.rem(tp + d, ntp)], share_in.at[d], on_tp(d))
        for d in range(1, ntp)
    ]

    def scatter(first, c, near, far, send, last, hops, kind, peer, number_of):
        near[1].wait_recv()
        near[7].wait_recv()
        for copy in far:
            copy.wait_recv()
        heads = [first[0, d, PG].astype(F32) for d in range(8)]

        def packet(e, out):
            wanted = number_of(e).astype(F32)
            total = jnp.zeros((PG, TILE, LANES), BF16)
            for d, head in enumerate(heads):
                mine = jnp.where(head == wanted, 1.0, 0.0).astype(BF16)[None]
                total = total + first[c, d, 0:PG] * mine
            out[...] = total

        sent = {}
        over = (2, 6)[c]
        for e, step, out in (
            (4, over, hops.at[c, 2]),
            (3, 1, hops.at[c, 0]),
            (5, 7, hops.at[c, 1]),
            (1, 1, last.at[c, 1]),
            (7, 7, last.at[c, 7]),
        ):
            packet(e, send.at[c, e])
            sent[e] = push(kind, e, send.at[c, e], out, peer(step))
        for e in (2, 6):
            packet(e, send.at[c, e])
        packet(0, last.at[c, 0])
        return sent

    def scatter_on(sent, c, send, last, hops, kind, peer):
        for e, came, hop in ((2, 3, 0), (6, 5, 1)):
            sent[came].wait_recv()
            total = send[c, e] + hops[c, hop]
            if e == (2, 6)[c]:
                sent[4].wait_recv()
                total = total + hops[c, 2]
            send[c, e] = total
            sent[e] = push(kind, e, send.at[c, e], last.at[c, e], peer(e))

    def number_z(e):
        return lax.rem(z + e, nz) * ny + y

    def number_y(e):
        return z * ny + lax.rem(y + e, ny)

    sent_a, sent_b = [], []

    def scatter_a(c):
        args = (first_a, c, near_a[c], far_a[c], send_a, last_a, hops_a)
        sent_a.append(scatter(*args, 4 + c, on_z, number_z))

    def scatter_b(c):
        args = (first_b, c, near_b[c], far_b[c], send_b, last_b, hops_b)
        sent_b.append(scatter(*args, 6 + c, on_y, number_y))

    scatter_a(0)

    hidden = share_out[tp]
    for d in range(1, ntp):
        sum_experts[d - 1].wait_recv()
        hidden = hidden + share_in[d]
    slot_no = lax.broadcasted_iota(jnp.int32, hidden.shape, 0)
    leaving = jnp.sum(jnp.where(slot_no == leave, hidden, 0.0), axis=0, keepdims=True)
    page_no = lax.shift_right_logical(len_ref[leave], 7)
    line = lax.broadcasted_iota(jnp.int32, (4, LANES), 0)
    row_y[0] = jnp.where(
        line == 0,
        leaving[:, 0:LANES],
        jnp.where(
            line == 1,
            leaving[:, LANES:],
            jnp.where(line == 2, target, page_no).astype(F32),
        ),
    )
    rows_y = [push(10, d, row_y.at[0], row_y.at[d], on_y(d)) for d in range(1, ny)]
    scatter_b(0)
    scatter_a(1)
    scatter_b(1)
    for copy in rows_y:
        copy.wait_recv()
    rows_z = []
    for e in range(nz):
        wanted = number_z(e).astype(F32)
        message = jnp.zeros((4, LANES), F32)
        for d in range(ny):
            one = row_y[d]
            message = message + jnp.where(one[2:3, :] == wanted, 1.0, 0.0) * one
        if e == 0:
            row_z[0] = message
        else:
            row_send[e] = message
            rows_z.append(push(11, e, row_send.at[e], row_z.at[e], on_z(e)))
    scatter_on(sent_a[0], 0, send_a, last_a, hops_a, 4, on_z)
    scatter_on(sent_b[0], 0, send_b, last_b, hops_b, 6, on_y)
    scatter_on(sent_a[1], 1, send_a, last_a, hops_a, 5, on_z)
    scatter_on(sent_b[1], 1, send_b, last_b, hops_b, 7, on_y)
    message = row_z[0]
    for e in range(1, nz):
        rows_z[e - 1].wait_recv()
        message = message + row_z[e]
    moved_row = jnp.concatenate([message[0:1, :], message[1:2, :]], axis=1)
    hidden = jnp.where(slot_no == leave, moved_row, hidden)
    hid_out[...] = hidden[0:REQ, 0:cols].astype(BF16)

    came_page = jnp.broadcast_to(message[3:4, :], (TILE, LANES))
    moved = jnp.zeros((PG, TILE, LANES), BF16)
    for c in range(2):
        for last, sent, p0 in ((last_a, sent_a, 0), (last_b, sent_b, 2)):
            page = last[c, 0]
            for e in (1, 7, 2, 6):
                sent[c][e].wait_recv()
                page = page + last[c, e]
            arr_out[p0 + c] = page.reshape(PAGE, LANES)
            mine = jnp.where(came_page == float(p0 + c), 1.0, 0.0).astype(BF16)
            moved = moved + page * mine[None]
    for r in range(REQ):
        kept = jnp.full((TILE, LANES), jnp.where(leave == r, 0.0, 1.0), F32)
        stays = cache[r, lax.shift_right_logical(len_ref[r], 7)].reshape(PG, TILE, LANES)
        page = stays * kept.astype(BF16)[None] + moved * (1.0 - kept).astype(BF16)[None]
        newp_out[r] = page.reshape(PAGE, LANES)

    for copies in (
        *(near.values() for near in near_a + near_b),
        *far_a,
        *far_b,
        sum_heads,
        sum_experts,
        *(sent.values() for sent in sent_a + sent_b),
        rows_y,
        rows_z,
    ):
        for copy in copies:
            copy.wait_send()


def write_out(hid, newp, arr, hid_hbm, newp_hbm, arr_hbm, sem):
    copies = [
        pltpu.make_async_copy(src, dst, sem.at[i])
        for i, (src, dst) in enumerate(((hid, hid_hbm), (newp, newp_hbm), (arr, arr_hbm)))
    ]
    for copy in copies:
        copy.start()
    for copy in copies:
        copy.wait()


def local(
    nz,
    ny,
    ntp,
    kv_pool,
    page_table,
    req_lengths,
    leave_slot,
    target_rep,
    qkv_new,
    residual_in,
    expert_ids,
    gate_weights,
    norm_gain,
    out_proj,
    expert_in,
    expert_down,
):
    width = residual_in.shape[1]
    cols = width // ntp
    most = max(nz, ny, ntp)
    vmem = pl.BlockSpec(memory_space=pltpu.VMEM)
    hbm = pl.BlockSpec(memory_space=pltpu.HBM)
    shapes = ((REQ, cols), (REQ, PAGE, LANES), (MAXP, PAGE, LANES))
    results = pl.pallas_call(
        functools.partial(kernel, nz, ny, ntp),
        out_shape=tuple(pltpu.VMEM(s, BF16) for s in shapes),
        in_specs=[hbm] * 13,
        out_specs=(vmem, vmem, vmem),
        scratch_shapes=[
            pltpu.SMEM(page_table.shape, jnp.int32),
            pltpu.SMEM(req_lengths.shape, jnp.int32),
            pltpu.SMEM(leave_slot.shape, jnp.int32),
            pltpu.SMEM(target_rep.shape, jnp.int32),
            pltpu.VMEM(qkv_new.shape, BF16),
            pltpu.VMEM(residual_in.shape, BF16),
            pltpu.VMEM(expert_ids.shape, jnp.int32),
            pltpu.VMEM(gate_weights.shape, BF16),
            pltpu.VMEM(norm_gain.shape, F32),
            pltpu.VMEM(kv_pool.shape, BF16),
            pltpu.VMEM(out_proj.shape, BF16),
            pltpu.VMEM(expert_in.shape[1:], BF16),
            pltpu.VMEM(expert_down.shape[1:], BF16),
            pltpu.VMEM((8, 3 * LANES), F32),
            pltpu.VMEM((8, LANES), F32),
            pltpu.VMEM((REQ, MAXP, PAGE, LANES), BF16),
            pltpu.VMEM((2, ny, PG + 1, TILE, LANES), BF16),
            pltpu.VMEM((2, nz, PG + 1, TILE, LANES), BF16),
            pltpu.VMEM((2, nz, PG, TILE, LANES), BF16),
            pltpu.VMEM((2, ny, PG, TILE, LANES), BF16),
            pltpu.VMEM((2, nz, PG, TILE, LANES), BF16),
            pltpu.VMEM((2, ny, PG, TILE, LANES), BF16),
            pltpu.VMEM((2, 3, PG, TILE, LANES), BF16),
            pltpu.VMEM((2, 3, PG, TILE, LANES), BF16),
            pltpu.VMEM((ntp, REQ, width), F32),
            pltpu.VMEM((8, width), F32),
            pltpu.VMEM((ntp, REQ, 2 * LANES), F32),
            pltpu.VMEM((ntp, REQ, 2 * LANES), F32),
            pltpu.VMEM((ny, 4, LANES), F32),
            pltpu.VMEM((nz, 4, LANES), F32),
            pltpu.VMEM((nz, 4, LANES), F32),
            pltpu.SemaphoreType.DMA((13,)),
            pltpu.SemaphoreType.DMA((12, most)),
            pltpu.SemaphoreType.DMA((12, most)),
            pltpu.SemaphoreType.REGULAR,
        ],
        compiler_params=pltpu.CompilerParams(
            collective_id=0, has_side_effects=True, vmem_limit_bytes=60 << 20
        ),
    )(
        page_table,
        req_lengths,
        leave_slot,
        target_rep,
        qkv_new,
        residual_in,
        expert_ids,
        gate_weights,
        norm_gain,
        kv_pool,
        out_proj,
        expert_in,
        expert_down,
    )
    return pl.pallas_call(
        write_out,
        out_shape=tuple(jax.ShapeDtypeStruct(s, BF16) for s in shapes),
        in_specs=[vmem] * 3,
        out_specs=[hbm] * 3,
        scratch_shapes=[pltpu.SemaphoreType.DMA((3,))],
        compiler_params=pltpu.CompilerParams(vmem_limit_bytes=1 << 20),
    )(*results)


def solution(mesh):
    nrep, ntp = mesh.shape["rep"], mesh.shape["tp"]
    ny = math.isqrt(nrep)
    return jax.shard_map(
        functools.partial(local, nrep // ny, ny, ntp),
        mesh=mesh,
        in_specs=(
            P("rep", None, "tp"),
            P("rep", None),
            P("rep"),
            P("rep"),
            P("rep"),
            P("rep", "tp"),
            P("rep", None),
            P("rep", None),
            P("rep", None),
            P(),
            P("tp", None),
            P("tp", None, None),
            P("tp", None, None),
        ),
        out_specs=(P("rep", "tp"), P("rep", None, "tp"), P("rep", None, "tp")),
        check_vma=False,
    )
```
